512 devices in a mesh: dp: 32 (over x, y, core), expert: 16 (over z).
Axes of the slice: x: 4, y: 4, z: 16, core: 2. Of those that a mesh axis runs over, the one named last changes fastest.
Arguments:
- tokens: bfloat16 [4096, 2048], P('dp', 'expert'), may hold values from -6 to 6
- cotangent: bfloat16 [4096, 2048], P('dp', 'expert'), may hold values from -6 to 6
- expert_ids: int32 [4096, 8], P('dp'), may hold values from 0 to 127, all different within a row; in each aligned block of 128 rows (0 to 127, 128 to 255, ...) at most 16 rows name the same one
- gate_weights: float32 [4096, 8], P('dp'), may hold values from 0.05 to 1
- w_gate: bfloat16 [512, 192, 2048], P(('dp', 'expert')), may hold values from -0.125 to 0.125
- w_up: bfloat16 [512, 192, 2048], P(('dp', 'expert')), may hold values from -0.125 to 0.125
- w_down: bfloat16 [512, 192, 2048], P(('dp', 'expert')), may hold values from -0.21875 to 0.21875
Outputs:
- layer_out: bfloat16 [4096, 2048], P('dp', 'expert')
- grad_tokens: bfloat16 [4096, 2048], P('dp', 'expert')
- grad_gates: float32 [4096, 8], P('dp')
- grad_w_gate: bfloat16 [512, 192, 2048], P(('dp', 'expert'))
- grad_w_up: bfloat16 [512, 192, 2048], P(('dp', 'expert'))
- grad_w_down: bfloat16 [512, 192, 2048], P(('dp', 'expert'))
The draws below stay inside these ranges and needn't reach their ends.
Inputs may be any that keep to these rules, and one draw needn't show every extreme that they name: `expert_ids`: each row names 8 different experts. In each aligned block of 128 rows (the rows of one index of dp) no expert is named by more than 16 rows, and in some block an expert is named by exactly 16 rows.
All inputs are finite; a program needn't handle non-finite values.
Results may differ from the reference program's by a relative error of at most 0.0064.
Values may be sent and summed in bfloat16 or wider, within the bound.
No kernel may reach another device: no remote copies, remote signals or barrier semaphores. Data moves between devices by JAX's collectives and lax.ppermute only.
A program may use at most 64 MiB of HBM per device.

```python
import math
import jax
import jax.numpy as jnp
import numpy as np
from jax import lax

D = 2048
FF = 768
TOP = 8
SHARDS = 4
TOK_DEV = 128
FFS = 192
EXPERTS = 128
TOKENS = 4096
CAP = 16
N_DP = 32


def shard_levels(stream_key, shape, cuts, least, high):
    def one(dim, parts):
        draws = jax.random.uniform(jax.random.fold_in(jax.random.fold_in(stream_key, 6), dim), (parts,), jnp.float32, least / len(cuts), high / len(cuts))
        return jnp.repeat(jnp.exp(draws), shape[dim] // parts).reshape((-1,) + (1,) * (len(shape) - dim - 1))

    factor_of = one(*cuts[0])
    for cut in cuts[1:]:
        factor_of = factor_of * one(*cut)
    return factor_of


def routed_block(stream_key, own, number, rows, amount, top, reach, skew):
    order = jax.random.permutation(stream_key, amount)
    crowded, ordinary = shares(amount, rows * top, reach, skew, True), shares(amount, rows * top, reach, skew, False)
    places = jnp.arange(amount)

    def named(lengths, offset_by):
        used = int((lengths > 0).sum())
        fixed = max(1, used // 4)
        passed = fixed + (places - fixed + offset_by * (used - fixed)) % max(1, amount - fixed)
        return jnp.zeros((amount,), jnp.int32).at[order[jnp.where(places < fixed, places, passed)]].set(jnp.asarray(lengths, jnp.int32))

    lengths = jnp.where(number % 4 == 0, named(crowded, number // 4), named(ordinary, number - number // 4 - 1))
    mixed = jax.random.permutation(jax.random.fold_in(own, 3), amount)
    source_of, sink = mixed[0:amount // 2 * 2:2], mixed[1:amount // 2 * 2:2]
    slack = jnp.minimum(lengths[source_of] - 1, reach - lengths[sink]) // 2
    slack = jnp.where((source_of == order[0]) | (sink == order[0]) | (lengths[sink] == 0), 0, jnp.maximum(slack, 0))
    passed = jax.random.randint(jax.random.fold_in(own, 4), (amount // 2,), 0, 1 << 20) % (slack + 1)
    lengths = lengths.at[source_of].add(-passed).at[sink].add(passed)
    members = jnp.searchsorted(jnp.cumsum(lengths), jnp.arange(rows * top), side="right").astype(jnp.int32)
    table = members.reshape(top, rows).T
    table = table[jax.random.permutation(jax.random.fold_in(own, 1), rows)]
    offset_by = jax.random.randint(jax.random.fold_in(own, 2), (rows, 1), 0, top)
    return jnp.take_along_axis(table, (jnp.arange(top)[None, :] + offset_by) % top, axis=1)


def shares(count, total, most, skew, full):
    weights = [(1 << 20) // math.isqrt(standing ** skew) + 1 for standing in range(1, count + 1)]
    largest = most if full else min(most, max(-(-total // count), total * weights[0] // sum(weights)))
    least = 1 if total - largest >= count - 1 else 0
    given, surplus = [largest] + [least] * (count - 1), total - largest - least * (count - 1)
    while surplus > 0:
        free = [i for i in range(1, count) if given[i] < largest] or [i for i in range(1, count) if given[i] < most]
        pool, remaining = sum([weights[i] for i in free]), surplus
        for i in free:
            addition = min(most - given[i], max(1, remaining * weights[i] // pool), surplus)
            given[i] = given[i] + addition
            surplus = surplus - addition
    return np.array(given)


def centred(stream_key, shape, spread, bound, split=(), kind=jnp.bfloat16):
    factor_of = shard_levels(stream_key, shape, split, -0.22, 0.18) if split else 1.0
    array = jax.random.normal(stream_key, shape, jnp.float32) * spread * factor_of
    return jnp.minimum(jnp.maximum(array, -bound), bound).astype(kind)


def setup_inputs(seed: int = 0) -> dict:
    arg_keys = jax.random.split(jax.random.key(seed), 8)
    tokens = centred(arg_keys[0], (TOKENS, D), 1.0, 6.0, ((0, 32), (1, 16)))
    cotangent = centred(arg_keys[1], (TOKENS, D), 1.0, 6.0, ((0, 32), (1, 16)))
    expert_ids_keys = jax.random.split(jax.random.fold_in(arg_keys[2], 1), TOKENS // TOK_DEV)
    expert_ids_turns = jax.random.permutation(jax.random.fold_in(arg_keys[2], 3), TOKENS // TOK_DEV)
    expert_ids = jax.vmap(lambda own, number: routed_block(jax.random.fold_in(arg_keys[2], 2), own, number, TOK_DEV, EXPERTS, TOP, CAP, 2))(expert_ids_keys, expert_ids_turns).reshape((TOKENS, TOP))
    gate_weights = jnp.clip(jnp.exp(math.log(1.0) - 2.9957323 * jax.random.uniform(arg_keys[3], (TOKENS, TOP), jnp.float32) ** shard_levels(arg_keys[3], (TOKENS, TOP), ((0, 32),), -0.2, 0.2)), 0.05, 1.0)
    w_gate = centred(arg_keys[4], (EXPERTS * SHARDS, FFS, D), D ** -0.5, 0.125, ((0, 512),))
    w_up = centred(arg_keys[5], (EXPERTS * SHARDS, FFS, D), D ** -0.5, 0.125, ((0, 512),))
    w_down = centred(arg_keys[6], (EXPERTS * SHARDS, FFS, D), FF ** -0.5, 0.21875, ((0, 512),))
    return dict(tokens=tokens, cotangent=cotangent, expert_ids=expert_ids, gate_weights=gate_weights, w_gate=w_gate, w_up=w_up, w_down=w_down)


def silu_parts(preact):
    sigmoid_of = jax.nn.sigmoid(preact)
    activated = preact * sigmoid_of
    derivative = sigmoid_of * (1.0 + preact * (1.0 - sigmoid_of))
    return activated, derivative


def reference(tokens, cotangent, expert_ids, gate_weights, w_gate, w_up, w_down):
    assigned = TOKENS * TOP
    slot_total = N_DP * CAP
    flat_ids = expert_ids.reshape(-1)
    flat_gates = gate_weights.reshape(-1)
    cot_float = cotangent.astype(jnp.float32)
    gate_all = w_gate.reshape(EXPERTS, SHARDS, FFS, D)
    up_all = w_up.reshape(EXPERTS, SHARDS, FFS, D)
    down_all = w_down.reshape(EXPERTS, SHARDS, FFS, D)

    def one_expert(carried, inputs):
        out_acc, grad_acc, gate_acc = carried
        expert_no, gate_w, up_w, down_w = inputs
        positions = jnp.nonzero(flat_ids == expert_no, size=slot_total, fill_value=assigned)[0].astype(jnp.int32)
        filled = positions < assigned
        safe_index = jnp.where(filled, positions, 0)
        row_token = safe_index // TOP
        gate_value = jnp.where(filled, flat_gates[safe_index], 0.0).astype(jnp.float32)
        rows_x = jnp.where(filled[:, None], tokens[row_token], jnp.zeros((), tokens.dtype))
        rows_dy = cot_float[row_token]
        rows_do = (gate_value[:, None] * rows_dy).astype(jnp.bfloat16)
        grads_gate = []
        grads_up = []
        grads_down = []
        for shard_at in range(SHARDS):
            pre_gate = jnp.dot(rows_x, gate_w[shard_at].T, preferred_element_type=jnp.float32)
            pre_up = jnp.dot(rows_x, up_w[shard_at].T, preferred_element_type=jnp.float32)
            activated, derivative = silu_parts(pre_gate)
            hidden = (activated * pre_up).astype(jnp.bfloat16)
            part_out = jnp.dot(hidden, down_w[shard_at], preferred_element_type=jnp.float32).astype(jnp.bfloat16)
            out_float = part_out.astype(jnp.float32)
            out_acc = out_acc.at[row_token].add(gate_value[:, None] * out_float)
            gate_acc = gate_acc.at[positions].add(jnp.sum(rows_dy * out_float, axis=1), mode="drop")
            d_hidden = jnp.dot(rows_do, down_w[shard_at].T, preferred_element_type=jnp.float32)
            d_pre_gate = (d_hidden * pre_up * derivative).astype(jnp.bfloat16)
            d_pre_up = (d_hidden * activated).astype(jnp.bfloat16)
            part_grad = (jnp.dot(d_pre_gate, gate_w[shard_at], preferred_element_type=jnp.float32)
                         + jnp.dot(d_pre_up, up_w[shard_at], preferred_element_type=jnp.float32)).astype(jnp.bfloat16)
            grad_acc = grad_acc.at[row_token].add(part_grad.astype(jnp.float32))
            grads_gate.append(jnp.dot(d_pre_gate.T, rows_x, preferred_element_type=jnp.float32).astype(jnp.bfloat16))
            grads_up.append(jnp.dot(d_pre_up.T, rows_x, preferred_element_type=jnp.float32).astype(jnp.bfloat16))
            grads_down.append(jnp.dot(hidden.T, rows_do, preferred_element_type=jnp.float32).astype(jnp.bfloat16))
        return (out_acc, grad_acc, gate_acc), (jnp.stack(grads_gate), jnp.stack(grads_up), jnp.stack(grads_down))

    initial = (jnp.zeros((TOKENS, D), jnp.float32), jnp.zeros((TOKENS, D), jnp.float32),
               jnp.zeros((assigned,), jnp.float32))
    numbers = jnp.arange(EXPERTS, dtype=jnp.int32)
    final, stacked = lax.scan(one_expert, initial, (numbers, gate_all, up_all, down_all))
    out_acc, grad_acc, gate_acc = final
    grad_w_gate = stacked[0].reshape(EXPERTS * SHARDS, FFS, D)
    grad_w_up = stacked[1].reshape(EXPERTS * SHARDS, FFS, D)
    grad_w_down = stacked[2].reshape(EXPERTS * SHARDS, FFS, D)
    return (out_acc.astype(jnp.bfloat16), grad_acc.astype(jnp.bfloat16), gate_acc.reshape(TOKENS, TOP),
            grad_w_gate, grad_w_up, grad_w_down)
```

```python
import jax
import jax.numpy as jnp
from jax import lax
from jax.sharding import PartitionSpec as P

SHARDS = 4


def silu_parts(preact):
    sigmoid_of = jax.nn.sigmoid(preact)
    activated = preact * sigmoid_of
    derivative = sigmoid_of * (1.0 + preact * (1.0 - sigmoid_of))
    return (activated, derivative)


def contract_last(first_op, second_op):
    return lax.dot_general(
        first_op, second_op, (((1,), (1,)), ((), ())), preferred_element_type=jnp.float32
    )


def contract_first(first_op, second_op):
    return lax.dot_general(
        first_op, second_op, (((0,), (0,)), ((), ())), preferred_element_type=jnp.float32
    )


def expert_rows(rows_x, rows_do, gate_w, up_w, down_w):
    pre_gate = contract_last(rows_x, gate_w)
    pre_up = contract_last(rows_x, up_w)
    activated, derivative = silu_parts(pre_gate)
    hidden = (activated * pre_up).astype(jnp.bfloat16)
    part_out = jnp.dot(hidden, down_w, preferred_element_type=jnp.float32).astype(jnp.bfloat16)
    d_hidden = contract_last(rows_do, down_w)
    d_pre_gate = (d_hidden * pre_up * derivative).astype(jnp.bfloat16)
    d_pre_up = (d_hidden * activated).astype(jnp.bfloat16)
    part_grad = (
        jnp.dot(d_pre_gate, gate_w, preferred_element_type=jnp.float32)
        + jnp.dot(d_pre_up, up_w, preferred_element_type=jnp.float32)
    ).astype(jnp.bfloat16)
    gradients = (
        contract_first(d_pre_gate, rows_x),
        contract_first(d_pre_up, rows_x),
        contract_first(hidden, rows_do),
    )
    return (part_out, part_grad, gradients)


def per_device(tokens, cotangent, expert_ids, gate_weights, w_gate, w_up, w_down):
    both = lax.all_gather(jnp.stack([tokens, cotangent]), "expert", axis=2, tiled=True)
    full_x, full_dy = both[0], both[1]
    dp_count = lax.axis_size("dp")
    column_count = lax.axis_size("expert")
    column = lax.axis_index("expert")
    tok_count, chosen = expert_ids.shape
    features = full_x.shape[1]
    experts_all = dp_count * column_count // SHARDS
    capacity = min(tok_count, max(2, 2 * tok_count * chosen // experts_all))
    per_row = column_count // SHARDS
    assigned = tok_count * chosen
    flat_ids = expert_ids.reshape(-1)
    flat_gates = gate_weights.reshape(-1)
    owned_here = flat_ids % per_row == column // SHARDS
    target_row = flat_ids // per_row
    onehot = (
        (target_row[:, None] == jnp.arange(dp_count, dtype=jnp.int32)[None, :])
        & owned_here[:, None]
    ).astype(jnp.int32)
    rank_of = jnp.sum((jnp.cumsum(onehot, axis=0) - 1) * onehot, axis=1)
    target = jnp.where(owned_here, target_row * capacity + rank_of, dp_count * capacity)
    slot_src = (
        jnp.full((dp_count * capacity,), assigned, jnp.int32)
        .at[target]
        .set(jnp.arange(assigned, dtype=jnp.int32), mode="drop")
    )
    filled = slot_src < assigned
    safe_index = jnp.where(filled, slot_src, 0)
    slot_token = safe_index // chosen
    slot_gate = jnp.where(filled, flat_gates[safe_index], 0.0)
    slot_dy = full_dy[slot_token].astype(jnp.float32)
    send_x = jnp.where(filled[:, None], full_x[slot_token], jnp.zeros((), full_x.dtype)).reshape(
        dp_count, capacity, features
    )
    send_do = (
        (slot_gate[:, None] * slot_dy).astype(jnp.bfloat16).reshape(dp_count, capacity, features)
    )
    weights = (w_gate[0], w_up[0], w_down[0])
    recv = lax.all_to_all(
        jnp.concatenate([send_x, send_do], axis=1), "dp", split_axis=0, concat_axis=0, tiled=True
    )
    rows_x = recv[:, :capacity].reshape(dp_count * capacity, features)
    rows_do = recv[:, capacity:].reshape(dp_count * capacity, features)
    part_out, part_grad, gradients = expert_rows(rows_x, rows_do, *weights)
    back = lax.all_to_all(
        jnp.concatenate(
            [
                part_out.reshape(dp_count, capacity, features),
                part_grad.reshape(dp_count, capacity, features),
            ],
            axis=1,
        ),
        "dp",
        split_axis=0,
        concat_axis=0,
        tiled=True,
    )
    out_float = back[:, :capacity].reshape(dp_count * capacity, features).astype(jnp.float32)
    grad_float = back[:, capacity:].reshape(dp_count * capacity, features).astype(jnp.float32)
    out_part = (
        jnp.zeros((tok_count, features), jnp.float32)
        .at[slot_token]
        .add(slot_gate[:, None] * out_float)
    )
    grad_part = jnp.zeros((tok_count, features), jnp.float32).at[slot_token].add(grad_float)
    gate_terms = jnp.sum(slot_dy * out_float, axis=1)
    gate_part = (
        jnp.zeros((assigned,), jnp.float32)
        .at[slot_src]
        .add(gate_terms, mode="drop")
        .reshape(tok_count, chosen)
    )
    summed = lax.psum_scatter(
        jnp.stack([out_part, grad_part]), "expert", scatter_dimension=2, tiled=True
    )
    grad_gates = lax.psum(gate_part, "expert")
    return (
        summed[0].astype(jnp.bfloat16),
        summed[1].astype(jnp.bfloat16),
        grad_gates,
        gradients[0].astype(jnp.bfloat16)[None],
        gradients[1].astype(jnp.bfloat16)[None],
        gradients[2].astype(jnp.bfloat16)[None],
    )


def solution(mesh):
    placed = (
        P("dp", "expert"),
        P("dp", "expert"),
        P("dp", None),
        P("dp", None),
        P(("dp", "expert"), None, None),
        P(("dp", "expert"), None, None),
        P(("dp", "expert"), None, None),
    )
    return jax.shard_map(
        per_device,
        mesh=mesh,
        in_specs=placed,
        out_specs=(
            P("dp", "expert"),
            P("dp", "expert"),
            P("dp", None),
            P(("dp", "expert"), None, None),
            P(("dp", "expert"), None, None),
            P(("dp", "expert"), None, None),
        ),
        check_vma=False,
    )
```

```python
import jax
import jax.numpy as jnp
from jax import lax
from jax.sharding import PartitionSpec as P

SHARDS = 4


def silu_parts(preact):
    sigmoid_of = jax.nn.sigmoid(preact)
    activated = preact * sigmoid_of
    derivative = sigmoid_of * (1.0 + preact * (1.0 - sigmoid_of))
    return (activated, derivative)


def contract_last(first_op, second_op):
    return lax.dot_general(
        first_op, second_op, (((1,), (1,)), ((), ())), preferred_element_type=jnp.float32
    )


def contract_first(first_op, second_op):
    return lax.dot_general(
        first_op, second_op, (((0,), (0,)), ((), ())), preferred_element_type=jnp.float32
    )


def expert_rows(rows_x, rows_do, gate_w, up_w, down_w):
    pre_gate = contract_last(rows_x, gate_w)
    pre_up = contract_last(rows_x, up_w)
    activated, derivative = silu_parts(pre_gate)
    hidden = (activated * pre_up).astype(jnp.bfloat16)
    part_out = jnp.dot(hidden, down_w, preferred_element_type=jnp.float32).astype(jnp.bfloat16)
    d_hidden = contract_last(rows_do, down_w)
    d_pre_gate = (d_hidden * pre_up * derivative).astype(jnp.bfloat16)
    d_pre_up = (d_hidden * activated).astype(jnp.bfloat16)
    part_grad = (
        jnp.dot(d_pre_gate, gate_w, preferred_element_type=jnp.float32)
        + jnp.dot(d_pre_up, up_w, preferred_element_type=jnp.float32)
    ).astype(jnp.bfloat16)
    gradients = (
        contract_first(d_pre_gate, rows_x),
        contract_first(d_pre_up, rows_x),
        contract_first(hidden, rows_do),
    )
    return (part_out, part_grad, gradients)


def per_device(tokens, cotangent, expert_ids, gate_weights, w_gate, w_up, w_down):
    both = lax.all_gather(jnp.stack([tokens, cotangent]), "expert", axis=2, tiled=True)
    full_x, full_dy = both[0], both[1]
    dp_count = lax.axis_size("dp")
    column_count = lax.axis_size("expert")
    column = lax.axis_index("expert")
    tok_count, chosen = expert_ids.shape
    features = full_x.shape[1]
    experts_all = dp_count * column_count // SHARDS
    capacity = min(tok_count, max(2, 2 * tok_count * chosen // experts_all))
    per_row = column_count // SHARDS
    assigned = tok_count * chosen
    flat_ids = expert_ids.reshape(-1)
    flat_gates = gate_weights.reshape(-1)
    slot_total = dp_count * capacity
    owned_here = flat_ids % per_row == column // SHARDS
    target_row = flat_ids // per_row
    onehot = (
        (target_row[:, None] == jnp.arange(dp_count, dtype=jnp.int32)[None, :])
        & owned_here[:, None]
    ).astype(jnp.bfloat16)
    order = jnp.arange(assigned, dtype=jnp.int32)
    earlier = (order[:, None] > order[None, :]).astype(jnp.bfloat16)
    counts = jnp.dot(earlier, onehot, preferred_element_type=jnp.float32)
    rank_of = jnp.sum(counts * onehot.astype(jnp.float32), axis=1).astype(jnp.int32)
    target = jnp.where(owned_here, target_row * capacity + rank_of, slot_total)
    picks = target[None, :] == jnp.arange(slot_total, dtype=jnp.int32)[:, None]
    slot_gate = jnp.sum(jnp.where(picks, flat_gates[None, :], 0.0), axis=1)
    token_of = jnp.any(picks.reshape(slot_total, tok_count, chosen), axis=2)
    token_pick = token_of.astype(jnp.bfloat16)
    send_x = jnp.dot(token_pick, full_x, preferred_element_type=jnp.bfloat16).reshape(
        dp_count, capacity, features
    )
    slot_dy = jnp.dot(token_pick, full_dy, preferred_element_type=jnp.float32)
    send_do = (
        (slot_gate[:, None] * slot_dy).astype(jnp.bfloat16).reshape(dp_count, capacity, features)
    )
    weights = (w_gate[0], w_up[0], w_down[0])
    recv = lax.all_to_all(
        jnp.concatenate([send_x, send_do], axis=1), "dp", split_axis=0, concat_axis=0, tiled=True
    )
    rows_x = recv[:, :capacity].reshape(dp_count * capacity, features)
    rows_do = recv[:, capacity:].reshape(dp_count * capacity, features)
    part_out, part_grad, gradients = expert_rows(rows_x, rows_do, *weights)
    back = lax.all_to_all(
        jnp.concatenate(
            [
                part_out.reshape(dp_count, capacity, features),
                part_grad.reshape(dp_count, capacity, features),
            ],
            axis=1,
        ),
        "dp",
        split_axis=0,
        concat_axis=0,
        tiled=True,
    )
    back_out = back[:, :capacity].reshape(slot_total, features)
    back_grad = back[:, capacity:].reshape(slot_total, features)
    gated_pick = token_pick.astype(jnp.float32) * slot_gate[:, None]
    out_part = lax.dot_general(
        gated_pick,
        back_out.astype(jnp.float32),
        (((0,), (0,)), ((), ())),
        precision=lax.Precision.HIGHEST,
        preferred_element_type=jnp.float32,
    )
    grad_part = contract_first(token_pick, back_grad)
    gate_terms = jnp.sum(slot_dy * back_out.astype(jnp.float32), axis=1)
    gate_part = jnp.sum(jnp.where(picks, gate_terms[:, None], 0.0), axis=0).reshape(
        tok_count, chosen
    )
    summed = lax.psum_scatter(
        jnp.stack([out_part, grad_part]), "expert", scatter_dimension=2, tiled=True
    )
    grad_gates = lax.psum(gate_part, "expert")
    return (
        summed[0].astype(jnp.bfloat16),
        summed[1].astype(jnp.bfloat16),
        grad_gates,
        gradients[0].astype(jnp.bfloat16)[None],
        gradients[1].astype(jnp.bfloat16)[None],
        gradients[2].astype(jnp.bfloat16)[None],
    )


def solution(mesh):
    placed = (
        P("dp", "expert"),
        P("dp", "expert"),
        P("dp", None),
        P("dp", None),
        P(("dp", "expert"), None, None),
        P(("dp", "expert"), None, None),
        P(("dp", "expert"), None, None),
    )
    return jax.shard_map(
        per_device,
        mesh=mesh,
        in_specs=placed,
        out_specs=(
            P("dp", "expert"),
            P("dp", "expert"),
            P("dp", None),
            P(("dp", "expert"), None, None),
            P(("dp", "expert"), None, None),
            P(("dp", "expert"), None, None),
        ),
        check_vma=False,
    )
```

```python
import jax
import jax.numpy as jnp
from jax import lax
from jax.sharding import PartitionSpec as P

SHARDS = 4


def silu_parts(preact):
    sigmoid_of = jax.nn.sigmoid(preact)
    activated = preact * sigmoid_of
    derivative = sigmoid_of * (1.0 + preact * (1.0 - sigmoid_of))
    return (activated, derivative)


def contract_last(first_op, second_op):
    return lax.dot_general(
        first_op, second_op, (((1,), (1,)), ((), ())), preferred_element_type=jnp.float32
    )


def contract_first(first_op, second_op):
    return lax.dot_general(
        first_op, second_op, (((0,), (0,)), ((), ())), preferred_element_type=jnp.float32
    )


def expert_rows(rows_x, rows_do, gate_w, up_w, down_w):
    pre_gate = contract_last(rows_x, gate_w)
    pre_up = contract_last(rows_x, up_w)
    activated, derivative = silu_parts(pre_gate)
    hidden = (activated * pre_up).astype(jnp.bfloat16)
    part_out = jnp.dot(hidden, down_w, preferred_element_type=jnp.float32).astype(jnp.bfloat16)
    d_hidden = contract_last(rows_do, down_w)
    d_pre_gate = (d_hidden * pre_up * derivative).astype(jnp.bfloat16)
    d_pre_up = (d_hidden * activated).astype(jnp.bfloat16)
    part_grad = (
        jnp.dot(d_pre_gate, gate_w, preferred_element_type=jnp.float32)
        + jnp.dot(d_pre_up, up_w, preferred_element_type=jnp.float32)
    ).astype(jnp.bfloat16)
    gradients = (
        contract_first(d_pre_gate, rows_x),
        contract_first(d_pre_up, rows_x),
        contract_first(hidden, rows_do),
    )
    return (part_out, part_grad, gradients)


def per_device(tokens, cotangent, expert_ids, gate_weights, w_gate, w_up, w_down):
    full_x = lax.all_gather(tokens, "expert", axis=1, tiled=True)
    full_dy = lax.all_gather(cotangent, "expert", axis=1, tiled=True)
    dp_count = lax.axis_size("dp")
    column_count = lax.axis_size("expert")
    column = lax.axis_index("expert")
    tok_count, chosen = expert_ids.shape
    features = full_x.shape[1]
    experts_all = dp_count * column_count // SHARDS
    capacity = min(tok_count, max(2, 2 * tok_count * chosen // experts_all))
    per_row = column_count // SHARDS
    assigned = tok_count * chosen
    flat_ids = expert_ids.reshape(-1)
    flat_gates = gate_weights.reshape(-1)
    slot_total = dp_count * capacity
    owned_here = flat_ids % per_row == column // SHARDS
    target_row = flat_ids // per_row
    onehot = (
        (target_row[:, None] == jnp.arange(dp_count, dtype=jnp.int32)[None, :])
        & owned_here[:, None]
    ).astype(jnp.bfloat16)
    order = jnp.arange(assigned, dtype=jnp.int32)
    earlier = (order[:, None] > order[None, :]).astype(jnp.bfloat16)
    counts = jnp.dot(earlier, onehot, preferred_element_type=jnp.float32)
    rank_of = jnp.sum(counts * onehot.astype(jnp.float32), axis=1).astype(jnp.int32)
    target = jnp.where(owned_here, target_row * capacity + rank_of, slot_total)
    picks = target[None, :] == jnp.arange(slot_total, dtype=jnp.int32)[:, None]
    slot_gate = jnp.sum(jnp.where(picks, flat_gates[None, :], 0.0), axis=1)
    token_of = jnp.any(picks.reshape(slot_total, tok_count, chosen), axis=2)
    token_pick = token_of.astype(jnp.bfloat16)
    send_x = jnp.dot(token_pick, full_x, preferred_element_type=jnp.bfloat16).reshape(
        dp_count, capacity, features
    )
    slot_dy = jnp.dot(token_pick, full_dy, preferred_element_type=jnp.float32)
    send_do = (
        (slot_gate[:, None] * slot_dy).astype(jnp.bfloat16).reshape(dp_count, capacity, features)
    )
    weights = (w_gate[0], w_up[0], w_down[0])
    recv = lax.all_to_all(
        jnp.concatenate([send_x, send_do], axis=1), "dp", split_axis=0, concat_axis=0, tiled=True
    )
    rows_x = recv[:, :capacity].reshape(dp_count * capacity, features)
    rows_do = recv[:, capacity:].reshape(dp_count * capacity, features)
    part_out, part_grad, gradients = expert_rows(rows_x, rows_do, *weights)
    back = lax.all_to_all(
        jnp.concatenate(
            [
                part_out.reshape(dp_count, capacity, features),
                part_grad.reshape(dp_count, capacity, features),
            ],
            axis=1,
        ),
        "dp",
        split_axis=0,
        concat_axis=0,
        tiled=True,
    )
    back_out = back[:, :capacity].reshape(slot_total, features)
    back_grad = back[:, capacity:].reshape(slot_total, features)
    gated_pick = token_pick.astype(jnp.float32) * slot_gate[:, None]
    out_part = lax.dot_general(
        gated_pick,
        back_out.astype(jnp.float32),
        (((0,), (0,)), ((), ())),
        precision=lax.Precision.HIGHEST,
        preferred_element_type=jnp.float32,
    )
    grad_part = contract_first(token_pick, back_grad)
    gate_terms = jnp.sum(slot_dy * back_out.astype(jnp.float32), axis=1)
    gate_part = jnp.sum(jnp.where(picks, gate_terms[:, None], 0.0), axis=0).reshape(
        tok_count, chosen
    )
    summed = lax.psum_scatter(
        jnp.stack([out_part, grad_part]), "expert", scatter_dimension=2, tiled=True
    )
    grad_gates = lax.psum(gate_part, "expert")
    return (
        summed[0].astype(jnp.bfloat16),
        summed[1].astype(jnp.bfloat16),
        grad_gates,
        gradients[0].astype(jnp.bfloat16)[None],
        gradients[1].astype(jnp.bfloat16)[None],
        gradients[2].astype(jnp.bfloat16)[None],
    )


def solution(mesh):
    placed = (
        P("dp", "expert"),
        P("dp", "expert"),
        P("dp", None),
        P("dp", None),
        P(("dp", "expert"), None, None),
        P(("dp", "expert"), None, None),
        P(("dp", "expert"), None, None),
    )
    return jax.shard_map(
        per_device,
        mesh=mesh,
        in_specs=placed,
        out_specs=(
            P("dp", "expert"),
            P("dp", "expert"),
            P("dp", None),
            P(("dp", "expert"), None, None),
            P(("dp", "expert"), None, None),
            P(("dp", "expert"), None, None),
        ),
        check_vma=False,
    )
```

```python
import jax
import jax.numpy as jnp
from jax import lax
from jax.experimental import pallas as pl
from jax.experimental.pallas import tpu as pltpu
from jax.sharding import PartitionSpec as P

SHARDS = 4


def silu_parts(preact):
    sigmoid_of = jax.nn.sigmoid(preact)
    activated = preact * sigmoid_of
    derivative = sigmoid_of * (1.0 + preact * (1.0 - sigmoid_of))
    return (activated, derivative)


def contract_last(first_op, second_op):
    return lax.dot_general(
        first_op, second_op, (((1,), (1,)), ((), ())), preferred_element_type=jnp.float32
    )


def contract_first(first_op, second_op):
    return lax.dot_general(
        first_op, second_op, (((0,), (0,)), ((), ())), preferred_element_type=jnp.float32
    )


def expert_rows(rows_x, rows_do, gate_w, up_w, down_w):
    pre_gate = contract_last(rows_x, gate_w)
    pre_up = contract_last(rows_x, up_w)
    activated, derivative = silu_parts(pre_gate)
    hidden = (activated * pre_up).astype(jnp.bfloat16)
    part_out = jnp.dot(hidden, down_w, preferred_element_type=jnp.float32).astype(jnp.bfloat16)
    d_hidden = contract_last(rows_do, down_w)
    d_pre_gate = (d_hidden * pre_up * derivative).astype(jnp.bfloat16)
    d_pre_up = (d_hidden * activated).astype(jnp.bfloat16)
    part_grad = (
        jnp.dot(d_pre_gate, gate_w, preferred_element_type=jnp.float32)
        + jnp.dot(d_pre_up, up_w, preferred_element_type=jnp.float32)
    ).astype(jnp.bfloat16)
    gradients = (
        contract_first(d_pre_gate, rows_x),
        contract_first(d_pre_up, rows_x),
        contract_first(hidden, rows_do),
    )
    return (part_out, part_grad, gradients)


def expert_kernel(recv_ref, gate_ref, up_ref, down_ref, back_ref, gw_ref, uw_ref, dw_ref,
                  acc_g, acc_u, acc_d):
    step = pl.program_id(0)
    sources, both, features = recv_ref.shape
    capacity = both // 2
    rows = sources * capacity
    x = recv_ref[:, :capacity, :].reshape(rows, features)
    do = recv_ref[:, capacity:, :].reshape(rows, features)
    gate_w = gate_ref[...]
    up_w = up_ref[...]
    down_w = down_ref[...]
    pre_gate = contract_last(x, gate_w)
    pre_up = contract_last(x, up_w)
    sigmoid_of = 1.0 / (1.0 + jnp.exp(-pre_gate))
    activated = pre_gate * sigmoid_of
    derivative = sigmoid_of * (1.0 + pre_gate * (1.0 - sigmoid_of))
    hidden = (activated * pre_up).astype(jnp.bfloat16)
    part_out = jnp.dot(hidden, down_w, preferred_element_type=jnp.float32)
    d_hidden = contract_last(do, down_w)
    d_pre_gate = (d_hidden * pre_up * derivative).astype(jnp.bfloat16)
    d_pre_up = (d_hidden * activated).astype(jnp.bfloat16)
    part_grad = jnp.dot(d_pre_gate, gate_w, preferred_element_type=jnp.float32) + jnp.dot(
        d_pre_up, up_w, preferred_element_type=jnp.float32
    )
    back_ref[:, :capacity, :] = part_out.astype(jnp.bfloat16).reshape(sources, capacity, features)
    back_ref[:, capacity:, :] = part_grad.astype(jnp.bfloat16).reshape(sources, capacity, features)

    @pl.when(step == 0)
    def _():
        acc_g[...] = jnp.zeros_like(acc_g)
        acc_u[...] = jnp.zeros_like(acc_u)
        acc_d[...] = jnp.zeros_like(acc_d)

    acc_g[...] += contract_first(d_pre_gate, x)
    acc_u[...] += contract_first(d_pre_up, x)
    acc_d[...] += contract_first(hidden, do)

    @pl.when(step == pl.num_programs(0) - 1)
    def _():
        gw_ref[...] = acc_g[...].astype(jnp.bfloat16)
        uw_ref[...] = acc_u[...].astype(jnp.bfloat16)
        dw_ref[...] = acc_d[...].astype(jnp.bfloat16)


def expert_call(recv, gate_w, up_w, down_w):
    dp_count, both, features = recv.shape
    hidden_units = gate_w.shape[0]
    per_step = 8
    weight_spec = pl.BlockSpec((hidden_units, features), lambda i: (0, 0))
    rows_spec = pl.BlockSpec((per_step, both, features), lambda i: (i, 0, 0))
    grad_shape = jax.ShapeDtypeStruct((hidden_units, features), jnp.bfloat16)
    return pl.pallas_call(
        expert_kernel,
        grid=(dp_count // per_step,),
        in_specs=[rows_spec, weight_spec, weight_spec, weight_spec],
        out_specs=[rows_spec, weight_spec, weight_spec, weight_spec],
        out_shape=[jax.ShapeDtypeStruct(recv.shape, jnp.bfloat16), grad_shape, grad_shape, grad_shape],
        scratch_shapes=[pltpu.VMEM((hidden_units, features), jnp.float32)] * 3,
        compiler_params=pltpu.CompilerParams(dimension_semantics=("arbitrary",)),
        name="expert_mlp",
    )(recv, gate_w, up_w, down_w)


def per_device(tokens, cotangent, expert_ids, gate_weights, w_gate, w_up, w_down):
    full_x = lax.all_gather(tokens, "expert", axis=1, tiled=True)
    full_dy = lax.all_gather(cotangent, "expert", axis=1, tiled=True)
    dp_count = lax.axis_size("dp")
    column_count = lax.axis_size("expert")
    column = lax.axis_index("expert")
    tok_count, chosen = expert_ids.shape
    features = full_x.shape[1]
    experts_all = dp_count * column_count // SHARDS
    capacity = min(tok_count, max(2, 2 * tok_count * chosen // experts_all))
    per_row = column_count // SHARDS
    assigned = tok_count * chosen
    flat_ids = expert_ids.reshape(-1)
    flat_gates = gate_weights.reshape(-1)
    slot_total = dp_count * capacity
    owned_here = flat_ids % per_row == column // SHARDS
    target_row = flat_ids // per_row
    onehot = (
        (target_row[:, None] == jnp.arange(dp_count, dtype=jnp.int32)[None, :])
        & owned_here[:, None]
    ).astype(jnp.bfloat16)
    order = jnp.arange(assigned, dtype=jnp.int32)
    earlier = (order[:, None] > order[None, :]).astype(jnp.bfloat16)
    counts = jnp.dot(earlier, onehot, preferred_element_type=jnp.float32)
    rank_of = jnp.sum(counts * onehot.astype(jnp.float32), axis=1).astype(jnp.int32)
    target = jnp.where(owned_here, target_row * capacity + rank_of, slot_total)
    picks = target[None, :] == jnp.arange(slot_total, dtype=jnp.int32)[:, None]
    slot_gate = jnp.sum(jnp.where(picks, flat_gates[None, :], 0.0), axis=1)
    token_of = jnp.any(picks.reshape(slot_total, tok_count, chosen), axis=2)
    token_pick = token_of.astype(jnp.bfloat16)
    send_x = jnp.dot(token_pick, full_x, preferred_element_type=jnp.bfloat16).reshape(
        dp_count, capacity, features
    )
    slot_dy = jnp.dot(token_pick, full_dy, preferred_element_type=jnp.float32)
    send_do = (
        (slot_gate[:, None] * slot_dy).astype(jnp.bfloat16).reshape(dp_count, capacity, features)
    )
    weights = (w_gate[0], w_up[0], w_down[0])
    recv = lax.all_to_all(
        jnp.concatenate([send_x, send_do], axis=1), "dp", split_axis=0, concat_axis=0, tiled=True
    )
    back, grad_gate_w, grad_up_w, grad_down_w = expert_call(recv, *weights)
    back = lax.all_to_all(back, "dp", split_axis=0, concat_axis=0, tiled=True)
    back_out = back[:, :capacity].reshape(slot_total, features)
    back_grad = back[:, capacity:].reshape(slot_total, features)
    gated_pick = token_pick.astype(jnp.float32) * slot_gate[:, None]
    out_part = lax.dot_general(
        gated_pick,
        back_out.astype(jnp.float32),
        (((0,), (0,)), ((), ())),
        precision=lax.Precision.HIGHEST,
        preferred_element_type=jnp.float32,
    )
    grad_part = contract_first(token_pick, back_grad)
    gate_terms = jnp.sum(slot_dy * back_out.astype(jnp.float32), axis=1)
    gate_part = jnp.sum(jnp.where(picks, gate_terms[:, None], 0.0), axis=0).reshape(
        tok_count, chosen
    )
    summed = lax.psum_scatter(
        jnp.stack([out_part, grad_part]), "expert", scatter_dimension=2, tiled=True
    )
    grad_gates = lax.psum(gate_part, "expert")
    return (
        summed[0].astype(jnp.bfloat16),
        summed[1].astype(jnp.bfloat16),
        grad_gates,
        grad_gate_w[None],
        grad_up_w[None],
        grad_down_w[None],
    )


def solution(mesh):
    placed = (
        P("dp", "expert"),
        P("dp", "expert"),
        P("dp", None),
        P("dp", None),
        P(("dp", "expert"), None, None),
        P(("dp", "expert"), None, None),
        P(("dp", "expert"), None, None),
    )
    return jax.shard_map(
        per_device,
        mesh=mesh,
        in_specs=placed,
        out_specs=(
            P("dp", "expert"),
            P("dp", "expert"),
            P("dp", None),
            P(("dp", "expert"), None, None),
            P(("dp", "expert"), None, None),
            P(("dp", "expert"), None, None),
        ),
        check_vma=False,
    )
```

```python
import jax
import jax.numpy as jnp
from jax import lax
from jax.sharding import PartitionSpec as P

SHARDS = 4


def silu_parts(preact):
    sigmoid_of = jax.nn.sigmoid(preact)
    activated = preact * sigmoid_of
    derivative = sigmoid_of * (1.0 + preact * (1.0 - sigmoid_of))
    return (activated, derivative)


def contract_last(first_op, second_op):
    return lax.dot_general(
        first_op, second_op, (((1,), (1,)), ((), ())), preferred_element_type=jnp.float32
    )


def contract_first(first_op, second_op):
    return lax.dot_general(
        first_op, second_op, (((0,), (0,)), ((), ())), preferred_element_type=jnp.float32
    )


def expert_rows(rows_x, rows_do, gate_w, up_w, down_w):
    pre_gate = contract_last(rows_x, gate_w)
    pre_up = contract_last(rows_x, up_w)
    activated, derivative = silu_parts(pre_gate)
    hidden = (activated * pre_up).astype(jnp.bfloat16)
    part_out = jnp.dot(hidden, down_w, preferred_element_type=jnp.float32).astype(jnp.bfloat16)
    d_hidden = contract_last(rows_do, down_w)
    d_pre_gate = (d_hidden * pre_up * derivative).astype(jnp.bfloat16)
    d_pre_up = (d_hidden * activated).astype(jnp.bfloat16)
    part_grad = (
        jnp.dot(d_pre_gate, gate_w, preferred_element_type=jnp.float32)
        + jnp.dot(d_pre_up, up_w, preferred_element_type=jnp.float32)
    ).astype(jnp.bfloat16)
    gradients = (
        contract_first(d_pre_gate, rows_x),
        contract_first(d_pre_up, rows_x),
        contract_first(hidden, rows_do),
    )
    return (part_out, part_grad, gradients)


def per_device(tokens, cotangent, expert_ids, gate_weights, w_gate, w_up, w_down):
    full_x = lax.all_gather(tokens, "expert", axis=1, tiled=True)
    full_dy = lax.all_gather(cotangent, "expert", axis=1, tiled=True)
    dp_count = lax.axis_size("dp")
    column_count = lax.axis_size("expert")
    column = lax.axis_index("expert")
    tok_count, chosen = expert_ids.shape
    features = full_x.shape[1]
    experts_all = dp_count * column_count // SHARDS
    capacity = min(tok_count, max(2, 2 * tok_count * chosen // experts_all))
    per_row = column_count // SHARDS
    assigned = tok_count * chosen
    flat_ids = expert_ids.reshape(-1)
    flat_gates = gate_weights.reshape(-1)
    slot_total = dp_count * capacity
    owned_here = flat_ids % per_row == column // SHARDS
    target_row = flat_ids // per_row
    onehot = (
        (target_row[:, None] == jnp.arange(dp_count, dtype=jnp.int32)[None, :])
        & owned_here[:, None]
    ).astype(jnp.bfloat16)
    order = jnp.arange(assigned, dtype=jnp.int32)
    earlier = (order[:, None] > order[None, :]).astype(jnp.bfloat16)
    counts = jnp.dot(earlier, onehot, preferred_element_type=jnp.float32)
    rank_of = jnp.sum(counts * onehot.astype(jnp.float32), axis=1).astype(jnp.int32)
    target = jnp.where(owned_here, target_row * capacity + rank_of, slot_total)
    picks = target[None, :] == jnp.arange(slot_total, dtype=jnp.int32)[:, None]
    slot_gate = jnp.sum(jnp.where(picks, flat_gates[None, :], 0.0), axis=1)
    token_of = jnp.any(picks.reshape(slot_total, tok_count, chosen), axis=2)
    token_pick = token_of.astype(jnp.bfloat16)
    send_x = jnp.dot(token_pick, full_x, preferred_element_type=jnp.bfloat16).reshape(
        dp_count, capacity, features
    )
    slot_dy = jnp.dot(token_pick, full_dy, preferred_element_type=jnp.float32)
    send_do = (
        (slot_gate[:, None] * slot_dy).astype(jnp.bfloat16).reshape(dp_count, capacity, features)
    )
    weights = (w_gate[0], w_up[0], w_down[0])
    recv_x = lax.all_to_all(send_x, "dp", split_axis=0, concat_axis=0, tiled=True)
    recv_do = lax.all_to_all(send_do, "dp", split_axis=0, concat_axis=0, tiled=True)
    rows_x = recv_x.reshape(slot_total, features)
    rows_do = recv_do.reshape(slot_total, features)
    part_out, part_grad, gradients = expert_rows(rows_x, rows_do, *weights)
    back = lax.all_to_all(
        jnp.concatenate(
            [
                part_out.reshape(dp_count, capacity, features),
                part_grad.reshape(dp_count, capacity, features),
            ],
            axis=1,
        ),
        "dp",
        split_axis=0,
        concat_axis=0,
        tiled=True,
    )
    back_out = back[:, :capacity].reshape(slot_total, features)
    back_grad = back[:, capacity:].reshape(slot_total, features)
    gated_pick = token_pick.astype(jnp.float32) * slot_gate[:, None]
    out_part = lax.dot_general(
        gated_pick,
        back_out.astype(jnp.float32),
        (((0,), (0,)), ((), ())),
        precision=lax.Precision.HIGHEST,
        preferred_element_type=jnp.float32,
    )
    grad_part = contract_first(token_pick, back_grad)
    gate_terms = jnp.sum(slot_dy * back_out.astype(jnp.float32), axis=1)
    gate_part = jnp.sum(jnp.where(picks, gate_terms[:, None], 0.0), axis=0).reshape(
        tok_count, chosen
    )
    summed = lax.psum_scatter(
        jnp.stack([out_part, grad_part]), "expert", scatter_dimension=2, tiled=True
    )
    grad_gates = lax.psum(gate_part, "expert")
    return (
        summed[0].astype(jnp.bfloat16),
        summed[1].astype(jnp.bfloat16),
        grad_gates,
        gradients[0].astype(jnp.bfloat16)[None],
        gradients[1].astype(jnp.bfloat16)[None],
        gradients[2].astype(jnp.bfloat16)[None],
    )


def solution(mesh):
    placed = (
        P("dp", "expert"),
        P("dp", "expert"),
        P("dp", None),
        P("dp", None),
        P(("dp", "expert"), None, None),
        P(("dp", "expert"), None, None),
        P(("dp", "expert"), None, None),
    )
    return jax.shard_map(
        per_device,
        mesh=mesh,
        in_specs=placed,
        out_specs=(
            P("dp", "expert"),
            P("dp", "expert"),
            P("dp", None),
            P(("dp", "expert"), None, None),
            P(("dp", "expert"), None, None),
            P(("dp", "expert"), None, None),
        ),
        check_vma=False,
    )
```

```python
import jax
import jax.numpy as jnp
from jax import lax
from jax.sharding import PartitionSpec as P

SHARDS = 4


def silu_parts(preact):
    sigmoid_of = jax.nn.sigmoid(preact)
    activated = preact * sigmoid_of
    derivative = sigmoid_of * (1.0 + preact * (1.0 - sigmoid_of))
    return (activated, derivative)


def contract_last(first_op, second_op):
    return lax.dot_general(
        first_op, second_op, (((1,), (1,)), ((), ())), preferred_element_type=jnp.float32
    )


def contract_first(first_op, second_op):
    return lax.dot_general(
        first_op, second_op, (((0,), (0,)), ((), ())), preferred_element_type=jnp.float32
    )


def expert_rows(rows_x, rows_do, gate_w, up_w, down_w):
    pre_gate = contract_last(rows_x, gate_w)
    pre_up = contract_last(rows_x, up_w)
    activated, derivative = silu_parts(pre_gate)
    hidden = (activated * pre_up).astype(jnp.bfloat16)
    part_out = jnp.dot(hidden, down_w, preferred_element_type=jnp.float32).astype(jnp.bfloat16)
    d_hidden = contract_last(rows_do, down_w)
    d_pre_gate = (d_hidden * pre_up * derivative).astype(jnp.bfloat16)
    d_pre_up = (d_hidden * activated).astype(jnp.bfloat16)
    part_grad = (
        jnp.dot(d_pre_gate, gate_w, preferred_element_type=jnp.float32)
        + jnp.dot(d_pre_up, up_w, preferred_element_type=jnp.float32)
    ).astype(jnp.bfloat16)
    gradients = (
        contract_first(d_pre_gate, rows_x),
        contract_first(d_pre_up, rows_x),
        contract_first(hidden, rows_do),
    )
    return (part_out, part_grad, gradients)


def per_device(tokens, cotangent, expert_ids, gate_weights, w_gate, w_up, w_down):
    full_x = lax.all_gather(tokens, "expert", axis=1, tiled=True)
    full_dy = lax.all_gather(cotangent, "expert", axis=1, tiled=True)
    dp_count = lax.axis_size("dp")
    column_count = lax.axis_size("expert")
    column = lax.axis_index("expert")
    tok_count, chosen = expert_ids.shape
    features = full_x.shape[1]
    experts_all = dp_count * column_count // SHARDS
    capacity = min(tok_count, max(2, 2 * tok_count * chosen // experts_all))
    per_row = column_count // SHARDS
    assigned = tok_count * chosen
    flat_ids = expert_ids.reshape(-1)
    flat_gates = gate_weights.reshape(-1)
    slot_total = dp_count * capacity
    owned_here = flat_ids % per_row == column // SHARDS
    target_row = flat_ids // per_row
    onehot = (
        (target_row[:, None] == jnp.arange(dp_count, dtype=jnp.int32)[None, :])
        & owned_here[:, None]
    ).astype(jnp.bfloat16)
    order = jnp.arange(assigned, dtype=jnp.int32)
    earlier = (order[:, None] > order[None, :]).astype(jnp.bfloat16)
    counts = jnp.dot(earlier, onehot, preferred_element_type=jnp.float32)
    rank_of = jnp.sum(counts * onehot.astype(jnp.float32), axis=1).astype(jnp.int32)
    target = jnp.where(owned_here, target_row * capacity + rank_of, slot_total)
    picks = target[None, :] == jnp.arange(slot_total, dtype=jnp.int32)[:, None]
    slot_gate = jnp.sum(jnp.where(picks, flat_gates[None, :], 0.0), axis=1)
    token_of = jnp.any(picks.reshape(slot_total, tok_count, chosen), axis=2)
    token_pick = token_of.astype(jnp.bfloat16)
    send_x = jnp.dot(token_pick, full_x, preferred_element_type=jnp.bfloat16).reshape(
        dp_count, capacity, features
    )
    slot_dy = jnp.dot(token_pick, full_dy, preferred_element_type=jnp.float32)
    send_do = (
        (slot_gate[:, None] * slot_dy).astype(jnp.bfloat16).reshape(dp_count, capacity, features)
    )
    weights = (w_gate[0], w_up[0], w_down[0])
    recv_x = lax.all_to_all(send_x, "dp", split_axis=0, concat_axis=0, tiled=True)
    recv_do = lax.all_to_all(send_do, "dp", split_axis=0, concat_axis=0, tiled=True)
    rows_x = recv_x.reshape(slot_total, features)
    rows_do = recv_do.reshape(slot_total, features)
    part_out, part_grad, gradients = expert_rows(rows_x, rows_do, *weights)
    back = lax.all_to_all(
        jnp.concatenate(
            [
                part_out.reshape(dp_count, capacity, features),
                part_grad.reshape(dp_count, capacity, features),
            ],
            axis=1,
        ),
        "dp",
        split_axis=0,
        concat_axis=0,
        tiled=True,
    )
    back_out = back[:, :capacity].reshape(slot_total, features)
    back_grad = back[:, capacity:].reshape(slot_total, features)
    gated_pick = token_pick.astype(jnp.float32) * slot_gate[:, None]
    out_part = lax.dot_general(
        gated_pick,
        back_out.astype(jnp.float32),
        (((0,), (0,)), ((), ())),
        precision=lax.Precision.HIGHEST,
        preferred_element_type=jnp.float32,
    )
    grad_part = contract_first(token_pick, back_grad)
    gate_terms = jnp.sum(slot_dy * back_out.astype(jnp.float32), axis=1)
    gate_part = jnp.sum(jnp.where(picks, gate_terms[:, None], 0.0), axis=0).reshape(
        tok_count, chosen
    )
    rounded = []
    rest = gate_part
    for _ in range(3):
        piece = lax.reduce_precision(rest, exponent_bits=8, mantissa_bits=7)
        rounded.append(piece)
        rest = rest - piece
    width = features // column_count
    parts = jnp.stack([out_part, grad_part]).astype(jnp.bfloat16)
    parts = parts.reshape(2, tok_count, column_count, width).transpose(2, 0, 1, 3)
    parts = parts.reshape(column_count, 2 * tok_count * width)
    gate_flat = jnp.stack(rounded).astype(jnp.bfloat16).reshape(1, 3 * tok_count * chosen)
    payload = jnp.concatenate(
        [parts, jnp.broadcast_to(gate_flat, (column_count, 3 * tok_count * chosen))], axis=1
    )
    arrived = lax.all_to_all(payload, "expert", split_axis=0, concat_axis=0, tiled=True)
    arrived = arrived.astype(jnp.float32)
    total = arrived[0]
    for source in range(1, column_count):
        total = total + arrived[source]
    summed = total[: 2 * tok_count * width].reshape(2, tok_count, width)
    gate_sums = total[2 * tok_count * width :].reshape(3, tok_count, chosen)
    grad_gates = (gate_sums[0] + gate_sums[1]) + gate_sums[2]
    return (
        summed[0].astype(jnp.bfloat16),
        summed[1].astype(jnp.bfloat16),
        grad_gates,
        gradients[0].astype(jnp.bfloat16)[None],
        gradients[1].astype(jnp.bfloat16)[None],
        gradients[2].astype(jnp.bfloat16)[None],
    )


def solution(mesh):
    placed = (
        P("dp", "expert"),
        P("dp", "expert"),
        P("dp", None),
        P("dp", None),
        P(("dp", "expert"), None, None),
        P(("dp", "expert"), None, None),
        P(("dp", "expert"), None, None),
    )
    return jax.shard_map(
        per_device,
        mesh=mesh,
        in_specs=placed,
        out_specs=(
            P("dp", "expert"),
            P("dp", "expert"),
            P("dp", None),
            P(("dp", "expert"), None, None),
            P(("dp", "expert"), None, None),
            P(("dp", "expert"), None, None),
        ),
        check_vma=False,
    )
```

```python
import jax
import jax.numpy as jnp
from jax import lax
from jax.experimental import pallas as pl
from jax.experimental.pallas import tpu as pltpu
from jax.sharding import PartitionSpec as P

SHARDS = 4


def silu_parts(preact):
    sigmoid_of = jax.nn.sigmoid(preact)
    activated = preact * sigmoid_of
    derivative = sigmoid_of * (1.0 + preact * (1.0 - sigmoid_of))
    return (activated, derivative)


def contract_last(first_op, second_op):
    return lax.dot_general(
        first_op, second_op, (((1,), (1,)), ((), ())), preferred_element_type=jnp.float32
    )


def contract_first(first_op, second_op):
    return lax.dot_general(
        first_op, second_op, (((0,), (0,)), ((), ())), preferred_element_type=jnp.float32
    )


def expert_rows(rows_x, rows_do, gate_w, up_w, down_w):
    pre_gate = contract_last(rows_x, gate_w)
    pre_up = contract_last(rows_x, up_w)
    activated, derivative = silu_parts(pre_gate)
    hidden = (activated * pre_up).astype(jnp.bfloat16)
    part_out = jnp.dot(hidden, down_w, preferred_element_type=jnp.float32).astype(jnp.bfloat16)
    d_hidden = contract_last(rows_do, down_w)
    d_pre_gate = (d_hidden * pre_up * derivative).astype(jnp.bfloat16)
    d_pre_up = (d_hidden * activated).astype(jnp.bfloat16)
    part_grad = (
        jnp.dot(d_pre_gate, gate_w, preferred_element_type=jnp.float32)
        + jnp.dot(d_pre_up, up_w, preferred_element_type=jnp.float32)
    ).astype(jnp.bfloat16)
    gradients = (
        contract_first(d_pre_gate, rows_x),
        contract_first(d_pre_up, rows_x),
        contract_first(hidden, rows_do),
    )
    return (part_out, part_grad, gradients)


def pick_kernel(pick_ref, scale_ref, rows_ref, out_ref):
    picked = jnp.dot(pick_ref[...], rows_ref[...], preferred_element_type=jnp.float32)
    out_ref[...] = (scale_ref[...] * picked).astype(out_ref.dtype)


def pick_rows(pick, scale, rows):
    slots, tokens = pick.shape
    features = rows.shape[1]
    block = 128
    return pl.pallas_call(
        pick_kernel,
        grid=(slots // block,),
        in_specs=[
            pl.BlockSpec((block, tokens), lambda i: (i, 0)),
            pl.BlockSpec((block, 1), lambda i: (i, 0)),
            pl.BlockSpec((tokens, features), lambda i: (0, 0)),
        ],
        out_specs=pl.BlockSpec((block, features), lambda i: (i, 0)),
        out_shape=jax.ShapeDtypeStruct((slots, features), jnp.bfloat16),
        compiler_params=pltpu.CompilerParams(dimension_semantics=("arbitrary",)),
        name="pick_rows",
    )(pick, scale, rows)


def per_device(tokens, cotangent, expert_ids, gate_weights, w_gate, w_up, w_down):
    full_x = lax.all_gather(tokens, "expert", axis=1, tiled=True)
    full_dy = lax.all_gather(cotangent, "expert", axis=1, tiled=True)
    dp_count = lax.axis_size("dp")
    column_count = lax.axis_size("expert")
    column = lax.axis_index("expert")
    tok_count, chosen = expert_ids.shape
    features = full_x.shape[1]
    experts_all = dp_count * column_count // SHARDS
    capacity = min(tok_count, max(2, 2 * tok_count * chosen // experts_all))
    per_row = column_count // SHARDS
    assigned = tok_count * chosen
    flat_ids = expert_ids.reshape(-1)
    flat_gates = gate_weights.reshape(-1)
    slot_total = dp_count * capacity
    owned_here = flat_ids % per_row == column // SHARDS
    target_row = flat_ids // per_row
    onehot = (
        (target_row[:, None] == jnp.arange(dp_count, dtype=jnp.int32)[None, :])
        & owned_here[:, None]
    ).astype(jnp.bfloat16)
    order = jnp.arange(assigned, dtype=jnp.int32)
    earlier = (order[:, None] > order[None, :]).astype(jnp.bfloat16)
    counts = jnp.dot(earlier, onehot, preferred_element_type=jnp.float32)
    rank_of = jnp.sum(counts * onehot.astype(jnp.float32), axis=1).astype(jnp.int32)
    target = jnp.where(owned_here, target_row * capacity + rank_of, slot_total)
    picks = target[None, :] == jnp.arange(slot_total, dtype=jnp.int32)[:, None]
    slot_gate = jnp.sum(jnp.where(picks, flat_gates[None, :], 0.0), axis=1)
    token_of = jnp.any(picks.reshape(slot_total, tok_count, chosen), axis=2)
    token_pick = token_of.astype(jnp.bfloat16)
    send_x = pick_rows(token_pick, jnp.ones((slot_total, 1), jnp.float32), full_x).reshape(
        dp_count, capacity, features
    )
    send_do = pick_rows(token_pick, slot_gate[:, None], full_dy).reshape(
        dp_count, capacity, features
    )
    weights = (w_gate[0], w_up[0], w_down[0])
    recv_x = lax.all_to_all(send_x, "dp", split_axis=0, concat_axis=0, tiled=True)
    recv_do = lax.all_to_all(send_do, "dp", split_axis=0, concat_axis=0, tiled=True)
    rows_x = recv_x.reshape(slot_total, features)
    rows_do = recv_do.reshape(slot_total, features)
    part_out, part_grad, gradients = expert_rows(rows_x, rows_do, *weights)
    back = lax.all_to_all(
        jnp.concatenate(
            [
                part_out.reshape(dp_count, capacity, features),
                part_grad.reshape(dp_count, capacity, features),
            ],
            axis=1,
        ),
        "dp",
        split_axis=0,
        concat_axis=0,
        tiled=True,
    )
    back_out = back[:, :capacity].reshape(slot_total, features)
    back_grad = back[:, capacity:].reshape(slot_total, features)
    gated_pick = token_pick.astype(jnp.float32) * slot_gate[:, None]
    out_part = lax.dot_general(
        gated_pick,
        back_out.astype(jnp.float32),
        (((0,), (0,)), ((), ())),
        precision=lax.Precision.HIGHEST,
        preferred_element_type=jnp.float32,
    )
    grad_part = contract_first(token_pick, back_grad)
    gate_terms = jnp.sum(
        token_pick.astype(jnp.float32) * contract_last(back_out, full_dy), axis=1
    )
    gate_part = jnp.sum(jnp.where(picks, gate_terms[:, None], 0.0), axis=0).reshape(
        tok_count, chosen
    )
    summed = lax.psum_scatter(
        jnp.stack([out_part, grad_part]), "expert", scatter_dimension=2, tiled=True
    )
    grad_gates = lax.psum(gate_part, "expert")
    return (
        summed[0].astype(jnp.bfloat16),
        summed[1].astype(jnp.bfloat16),
        grad_gates,
        gradients[0].astype(jnp.bfloat16)[None],
        gradients[1].astype(jnp.bfloat16)[None],
        gradients[2].astype(jnp.bfloat16)[None],
    )


def solution(mesh):
    placed = (
        P("dp", "expert"),
        P("dp", "expert"),
        P("dp", None),
        P("dp", None),
        P(("dp", "expert"), None, None),
        P(("dp", "expert"), None, None),
        P(("dp", "expert"), None, None),
    )
    return jax.shard_map(
        per_device,
        mesh=mesh,
        in_specs=placed,
        out_specs=(
            P("dp", "expert"),
            P("dp", "expert"),
            P("dp", None),
            P(("dp", "expert"), None, None),
            P(("dp", "expert"), None, None),
            P(("dp", "expert"), None, None),
        ),
        check_vma=False,
    )
```

```python
import jax
import jax.numpy as jnp
from jax import lax
from jax.sharding import PartitionSpec as P

SHARDS = 4


def silu_parts(preact):
    sigmoid_of = jax.nn.sigmoid(preact)
    activated = preact * sigmoid_of
    derivative = sigmoid_of * (1.0 + preact * (1.0 - sigmoid_of))
    return (activated, derivative)


def contract_last(first_op, second_op):
    return lax.dot_general(
        first_op, second_op, (((1,), (1,)), ((), ())), preferred_element_type=jnp.float32
    )


def contract_first(first_op, second_op):
    return lax.dot_general(
        first_op, second_op, (((0,), (0,)), ((), ())), preferred_element_type=jnp.float32
    )


def expert_rows(rows_x, rows_do, gate_w, up_w, down_w):
    pre_gate = contract_last(rows_x, gate_w)
    pre_up = contract_last(rows_x, up_w)
    activated, derivative = silu_parts(pre_gate)
    hidden = (activated * pre_up).astype(jnp.bfloat16)
    part_out = jnp.dot(hidden, down_w, preferred_element_type=jnp.float32).astype(jnp.bfloat16)
    d_hidden = contract_last(rows_do, down_w)
    d_pre_gate = (d_hidden * pre_up * derivative).astype(jnp.bfloat16)
    d_pre_up = (d_hidden * activated).astype(jnp.bfloat16)
    part_grad = (
        jnp.dot(d_pre_gate, gate_w, preferred_element_type=jnp.float32)
        + jnp.dot(d_pre_up, up_w, preferred_element_type=jnp.float32)
    ).astype(jnp.bfloat16)
    gradients = (
        contract_first(d_pre_gate, rows_x),
        contract_first(d_pre_up, rows_x),
        contract_first(hidden, rows_do),
    )
    return (part_out, part_grad, gradients)


def per_device(tokens, cotangent, expert_ids, gate_weights, w_gate, w_up, w_down):
    full_x = lax.all_gather(tokens, "expert", axis=1, tiled=True)
    full_dy = lax.all_gather(cotangent, "expert", axis=1, tiled=True)
    dp_count = lax.axis_size("dp")
    column_count = lax.axis_size("expert")
    column = lax.axis_index("expert")
    tok_count, chosen = expert_ids.shape
    features = full_x.shape[1]
    experts_all = dp_count * column_count // SHARDS
    capacity = min(tok_count, max(2, 2 * tok_count * chosen // experts_all))
    per_row = column_count // SHARDS
    assigned = tok_count * chosen
    flat_ids = expert_ids.reshape(-1)
    flat_gates = gate_weights.reshape(-1)
    slot_total = dp_count * capacity
    owned_here = flat_ids % per_row == column // SHARDS
    target_row = flat_ids // per_row
    onehot = (
        (target_row[:, None] == jnp.arange(dp_count, dtype=jnp.int32)[None, :])
        & owned_here[:, None]
    ).astype(jnp.bfloat16)
    order = jnp.arange(assigned, dtype=jnp.int32)
    earlier = (order[:, None] > order[None, :]).astype(jnp.bfloat16)
    counts = jnp.dot(earlier, onehot, preferred_element_type=jnp.float32)
    rank_of = jnp.sum(counts * onehot.astype(jnp.float32), axis=1).astype(jnp.int32)
    target = jnp.where(owned_here, target_row * capacity + rank_of, slot_total)
    picks = target[None, :] == jnp.arange(slot_total, dtype=jnp.int32)[:, None]
    slot_gate = jnp.sum(jnp.where(picks, flat_gates[None, :], 0.0), axis=1)
    token_of = jnp.any(picks.reshape(slot_total, tok_count, chosen), axis=2)
    token_pick = token_of.astype(jnp.bfloat16)
    send_x = jnp.dot(token_pick, full_x, preferred_element_type=jnp.bfloat16).reshape(
        dp_count, capacity, features
    )
    slot_dy = jnp.dot(token_pick, full_dy, preferred_element_type=jnp.float32)
    send_do = (
        (slot_gate[:, None] * slot_dy).astype(jnp.bfloat16).reshape(dp_count, capacity, features)
    )
    weights = (w_gate[0], w_up[0], w_down[0])
    recv_x = lax.all_to_all(send_x, "dp", split_axis=0, concat_axis=0, tiled=True)
    recv_do = lax.all_to_all(send_do, "dp", split_axis=0, concat_axis=0, tiled=True)
    rows_x = recv_x.reshape(slot_total, features)
    rows_do = recv_do.reshape(slot_total, features)
    part_out, part_grad, gradients = expert_rows(rows_x, rows_do, *weights)
    back = lax.all_to_all(
        jnp.concatenate(
            [
                part_out.reshape(dp_count, capacity, features),
                part_grad.reshape(dp_count, capacity, features),
            ],
            axis=1,
        ),
        "dp",
        split_axis=0,
        concat_axis=0,
        tiled=True,
    )
    back_out = back[:, :capacity].reshape(slot_total, features)
    back_grad = back[:, capacity:].reshape(slot_total, features)
    gated_pick = token_pick.astype(jnp.float32) * slot_gate[:, None]
    out_part = lax.dot_general(
        gated_pick,
        back_out.astype(jnp.float32),
        (((0,), (0,)), ((), ())),
        precision=lax.Precision.HIGHEST,
        preferred_element_type=jnp.float32,
    )
    grad_part = contract_first(token_pick, back_grad)
    gate_terms = jnp.sum(
        token_pick.astype(jnp.float32) * contract_last(back_out, full_dy), axis=1
    )
    gate_part = jnp.sum(jnp.where(picks, gate_terms[:, None], 0.0), axis=0).reshape(
        tok_count, chosen
    )
    summed = lax.psum_scatter(
        jnp.stack([out_part, grad_part]), "expert", scatter_dimension=2, tiled=True
    )
    grad_gates = lax.psum(gate_part, "expert")
    return (
        summed[0].astype(jnp.bfloat16),
        summed[1].astype(jnp.bfloat16),
        grad_gates,
        gradients[0].astype(jnp.bfloat16)[None],
        gradients[1].astype(jnp.bfloat16)[None],
        gradients[2].astype(jnp.bfloat16)[None],
    )


def solution(mesh):
    placed = (
        P("dp", "expert"),
        P("dp", "expert"),
        P("dp", None),
        P("dp", None),
        P(("dp", "expert"), None, None),
        P(("dp", "expert"), None, None),
        P(("dp", "expert"), None, None),
    )
    return jax.shard_map(
        per_device,
        mesh=mesh,
        in_specs=placed,
        out_specs=(
            P("dp", "expert"),
            P("dp", "expert"),
            P("dp", None),
            P(("dp", "expert"), None, None),
            P(("dp", "expert"), None, None),
            P(("dp", "expert"), None, None),
        ),
        check_vma=False,
    )
```

```python
import jax
import jax.numpy as jnp
from jax import lax
from jax.sharding import PartitionSpec as P

SHARDS = 4


def silu_parts(preact):
    sigmoid_of = jax.nn.sigmoid(preact)
    activated = preact * sigmoid_of
    derivative = sigmoid_of * (1.0 + preact * (1.0 - sigmoid_of))
    return (activated, derivative)


def contract_last(first_op, second_op):
    return lax.dot_general(
        first_op, second_op, (((1,), (1,)), ((), ())), preferred_element_type=jnp.float32
    )


def contract_first(first_op, second_op):
    return lax.dot_general(
        first_op, second_op, (((0,), (0,)), ((), ())), preferred_element_type=jnp.float32
    )


def expert_rows(rows_x, rows_do, gate_w, up_w, down_w):
    pre_gate = contract_last(rows_x, gate_w)
    pre_up = contract_last(rows_x, up_w)
    activated, derivative = silu_parts(pre_gate)
    hidden = (activated * pre_up).astype(jnp.bfloat16)
    part_out = jnp.dot(hidden, down_w, preferred_element_type=jnp.float32).astype(jnp.bfloat16)
    d_hidden = contract_last(rows_do, down_w)
    d_pre_gate = (d_hidden * pre_up * derivative).astype(jnp.bfloat16)
    d_pre_up = (d_hidden * activated).astype(jnp.bfloat16)
    part_grad = (
        jnp.dot(d_pre_gate, gate_w, preferred_element_type=jnp.float32)
        + jnp.dot(d_pre_up, up_w, preferred_element_type=jnp.float32)
    ).astype(jnp.bfloat16)
    gradients = (
        contract_first(d_pre_gate, rows_x),
        contract_first(d_pre_up, rows_x),
        contract_first(hidden, rows_do),
    )
    return (part_out, part_grad, gradients)


def per_device(tokens, cotangent, expert_ids, gate_weights, w_gate, w_up, w_down):
    full_x = lax.all_gather(tokens, "expert", axis=1, tiled=True)
    full_dy = lax.all_gather(cotangent, "expert", axis=1, tiled=True)
    dp_count = lax.axis_size("dp")
    column_count = lax.axis_size("expert")
    column = lax.axis_index("expert")
    tok_count, chosen = expert_ids.shape
    features = full_x.shape[1]
    experts_all = dp_count * column_count // SHARDS
    capacity = min(tok_count, max(2, 2 * tok_count * chosen // experts_all))
    per_row = column_count // SHARDS
    assigned = tok_count * chosen
    flat_ids = expert_ids.reshape(-1)
    flat_gates = gate_weights.reshape(-1)
    slot_total = dp_count * capacity
    owned_here = flat_ids % per_row == column // SHARDS
    target_row = flat_ids // per_row
    onehot = (
        (target_row[:, None] == jnp.arange(dp_count, dtype=jnp.int32)[None, :])
        & owned_here[:, None]
    ).astype(jnp.bfloat16)
    order = jnp.arange(assigned, dtype=jnp.int32)
    earlier = (order[:, None] > order[None, :]).astype(jnp.bfloat16)
    counts = jnp.dot(earlier, onehot, preferred_element_type=jnp.float32)
    rank_of = jnp.sum(counts * onehot.astype(jnp.float32), axis=1).astype(jnp.int32)
    target = jnp.where(owned_here, target_row * capacity + rank_of, slot_total)
    picks = target[None, :] == jnp.arange(slot_total, dtype=jnp.int32)[:, None]
    slot_gate = jnp.sum(jnp.where(picks, flat_gates[None, :], 0.0), axis=1)
    token_of = jnp.any(picks.reshape(slot_total, tok_count, chosen), axis=2)
    token_pick = token_of.astype(jnp.bfloat16)
    send_x = jnp.dot(token_pick, full_x, preferred_element_type=jnp.bfloat16).reshape(
        dp_count, capacity, features
    )
    slot_dy = jnp.dot(token_pick, full_dy, preferred_element_type=jnp.float32)
    send_do = (
        (slot_gate[:, None] * slot_dy).astype(jnp.bfloat16).reshape(dp_count, capacity, features)
    )
    weights = (w_gate[0], w_up[0], w_down[0])
    recv_x = lax.all_to_all(send_x, "dp", split_axis=0, concat_axis=0, tiled=True)
    recv_do = lax.all_to_all(send_do, "dp", split_axis=0, concat_axis=0, tiled=True)
    rows_x = recv_x.reshape(slot_total, features)
    rows_do = recv_do.reshape(slot_total, features)
    part_out, part_grad, gradients = expert_rows(rows_x, rows_do, *weights)
    back = lax.all_to_all(
        jnp.concatenate(
            [
                part_out.reshape(dp_count, capacity, features),
                part_grad.reshape(dp_count, capacity, features),
            ],
            axis=1,
        ),
        "dp",
        split_axis=0,
        concat_axis=0,
        tiled=True,
    )
    back_out = back[:, :capacity].reshape(slot_total, features)
    back_grad = back[:, capacity:].reshape(slot_total, features)
    gated_pick = token_pick.astype(jnp.float32) * slot_gate[:, None]
    out_part = lax.dot_general(
        gated_pick,
        back_out.astype(jnp.float32),
        (((0,), (0,)), ((), ())),
        precision=lax.Precision.HIGHEST,
        preferred_element_type=jnp.float32,
    )
    grad_part = contract_first(token_pick, back_grad)
    gate_terms = jnp.sum(slot_dy * back_out.astype(jnp.float32), axis=1)
    gate_part = jnp.sum(jnp.where(picks, gate_terms[:, None], 0.0), axis=0).reshape(
        tok_count, chosen
    )
    summed = lax.psum_scatter(
        jnp.stack([out_part, grad_part]), "expert", scatter_dimension=2, tiled=True
    )
    gate_all = lax.all_gather(gate_part, "expert", axis=0, tiled=False)
    grad_gates = gate_all[0]
    for source in range(1, column_count):
        grad_gates = grad_gates + gate_all[source]
    return (
        summed[0].astype(jnp.bfloat16),
        summed[1].astype(jnp.bfloat16),
        grad_gates,
        gradients[0].astype(jnp.bfloat16)[None],
        gradients[1].astype(jnp.bfloat16)[None],
        gradients[2].astype(jnp.bfloat16)[None],
    )


def solution(mesh):
    placed = (
        P("dp", "expert"),
        P("dp", "expert"),
        P("dp", None),
        P("dp", None),
        P(("dp", "expert"), None, None),
        P(("dp", "expert"), None, None),
        P(("dp", "expert"), None, None),
    )
    return jax.shard_map(
        per_device,
        mesh=mesh,
        in_specs=placed,
        out_specs=(
            P("dp", "expert"),
            P("dp", "expert"),
            P("dp", None),
            P(("dp", "expert"), None, None),
            P(("dp", "expert"), None, None),
            P(("dp", "expert"), None, None),
        ),
        check_vma=False,
    )
```

```python
import jax
import jax.numpy as jnp
from jax import lax
from jax.sharding import PartitionSpec as P

SHARDS = 4


def silu_parts(preact):
    sigmoid_of = jax.nn.sigmoid(preact)
    activated = preact * sigmoid_of
    derivative = sigmoid_of * (1.0 + preact * (1.0 - sigmoid_of))
    return (activated, derivative)


def contract_last(first_op, second_op):
    return lax.dot_general(
        first_op, second_op, (((1,), (1,)), ((), ())), preferred_element_type=jnp.float32
    )


def contract_first(first_op, second_op):
    return lax.dot_general(
        first_op, second_op, (((0,), (0,)), ((), ())), preferred_element_type=jnp.float32
    )


def expert_rows(rows_x, rows_do, gate_w, up_w, down_w):
    pre_gate = contract_last(rows_x, gate_w)
    pre_up = contract_last(rows_x, up_w)
    activated, derivative = silu_parts(pre_gate)
    hidden = (activated * pre_up).astype(jnp.bfloat16)
    part_out = jnp.dot(hidden, down_w, preferred_element_type=jnp.float32).astype(jnp.bfloat16)
    d_hidden = contract_last(rows_do, down_w)
    d_pre_gate = (d_hidden * pre_up * derivative).astype(jnp.bfloat16)
    d_pre_up = (d_hidden * activated).astype(jnp.bfloat16)
    part_grad = (
        jnp.dot(d_pre_gate, gate_w, preferred_element_type=jnp.float32)
        + jnp.dot(d_pre_up, up_w, preferred_element_type=jnp.float32)
    ).astype(jnp.bfloat16)
    gradients = (
        contract_first(d_pre_gate, rows_x),
        contract_first(d_pre_up, rows_x),
        contract_first(hidden, rows_do),
    )
    return (part_out, part_grad, gradients)


def per_device(tokens, cotangent, expert_ids, gate_weights, w_gate, w_up, w_down):
    full_x = lax.all_gather(tokens, "expert", axis=1, tiled=True)
    full_dy = lax.all_gather(cotangent, "expert", axis=1, tiled=True)
    dp_count = lax.axis_size("dp")
    column_count = lax.axis_size("expert")
    column = lax.axis_index("expert")
    tok_count, chosen = expert_ids.shape
    features = full_x.shape[1]
    experts_all = dp_count * column_count // SHARDS
    capacity = min(tok_count, max(2, 2 * tok_count * chosen // experts_all))
    per_row = column_count // SHARDS
    assigned = tok_count * chosen
    flat_ids = expert_ids.reshape(-1)
    flat_gates = gate_weights.reshape(-1)
    slot_total = dp_count * capacity
    owned_here = flat_ids % per_row == column // SHARDS
    target_row = flat_ids // per_row
    onehot = (
        (target_row[:, None] == jnp.arange(dp_count, dtype=jnp.int32)[None, :])
        & owned_here[:, None]
    ).astype(jnp.bfloat16)
    order = jnp.arange(assigned, dtype=jnp.int32)
    earlier = (order[:, None] > order[None, :]).astype(jnp.bfloat16)
    counts = jnp.dot(earlier, onehot, preferred_element_type=jnp.float32)
    rank_of = jnp.sum(counts * onehot.astype(jnp.float32), axis=1).astype(jnp.int32)
    target = jnp.where(owned_here, target_row * capacity + rank_of, slot_total)
    picks = target[None, :] == jnp.arange(slot_total, dtype=jnp.int32)[:, None]
    slot_gate = jnp.sum(jnp.where(picks, flat_gates[None, :], 0.0), axis=1)
    token_of = jnp.any(picks.reshape(slot_total, tok_count, chosen), axis=2)
    token_pick = token_of.astype(jnp.bfloat16)
    send_x = jnp.dot(token_pick, full_x, preferred_element_type=jnp.bfloat16).reshape(
        dp_count, capacity, features
    )
    slot_dy = jnp.dot(token_pick, full_dy, preferred_element_type=jnp.float32)
    send_do = (
        (slot_gate[:, None] * slot_dy).astype(jnp.bfloat16).reshape(dp_count, capacity, features)
    )
    weights = (w_gate[0], w_up[0], w_down[0])
    recv_x = lax.all_to_all(send_x, "dp", split_axis=0, concat_axis=0, tiled=True)
    recv_do = lax.all_to_all(send_do, "dp", split_axis=0, concat_axis=0, tiled=True)
    rows_x = recv_x.reshape(slot_total, features)
    rows_do = recv_do.reshape(slot_total, features)
    part_out, part_grad, gradients = expert_rows(rows_x, rows_do, *weights)
    back = lax.all_to_all(
        jnp.concatenate(
            [
                part_out.reshape(dp_count, capacity, features),
                part_grad.reshape(dp_count, capacity, features),
            ],
            axis=1,
        ),
        "dp",
        split_axis=0,
        concat_axis=0,
        tiled=True,
    )
    back_out = back[:, :capacity].reshape(slot_total, features)
    back_grad = back[:, capacity:].reshape(slot_total, features)
    gated_pick = token_pick.astype(jnp.float32) * slot_gate[:, None]
    out_part = lax.dot_general(
        gated_pick,
        back_out.astype(jnp.float32),
        (((0,), (0,)), ((), ())),
        precision=lax.Precision.HIGHEST,
        preferred_element_type=jnp.float32,
    )
    grad_part = contract_first(token_pick, back_grad)
    gate_terms = jnp.sum(slot_dy * back_out.astype(jnp.float32), axis=1)
    gate_part = jnp.sum(jnp.where(picks, gate_terms[:, None], 0.0), axis=0).reshape(
        tok_count, chosen
    )
    group = SHARDS
    outer = column_count // group
    width = features // column_count
    stacked = jnp.stack([out_part, grad_part]).reshape(2, tok_count, outer, group, width)
    stacked = stacked.transpose(0, 1, 3, 2, 4).reshape(2, tok_count, features)
    near = [[g * group + i for i in range(group)] for g in range(outer)]
    far = [[g * group + i for g in range(outer)] for i in range(group)]
    summed = lax.psum_scatter(
        stacked, "expert", scatter_dimension=2, axis_index_groups=near, tiled=True
    )
    summed = lax.psum_scatter(
        summed, "expert", scatter_dimension=2, axis_index_groups=far, tiled=True
    )
    gate_all = lax.all_gather(gate_part, "expert", axis=0, tiled=False)
    grad_gates = gate_all[0]
    for source in range(1, column_count):
        grad_gates = grad_gates + gate_all[source]
    return (
        summed[0].astype(jnp.bfloat16),
        summed[1].astype(jnp.bfloat16),
        grad_gates,
        gradients[0].astype(jnp.bfloat16)[None],
        gradients[1].astype(jnp.bfloat16)[None],
        gradients[2].astype(jnp.bfloat16)[None],
    )


def solution(mesh):
    placed = (
        P("dp", "expert"),
        P("dp", "expert"),
        P("dp", None),
        P("dp", None),
        P(("dp", "expert"), None, None),
        P(("dp", "expert"), None, None),
        P(("dp", "expert"), None, None),
    )
    return jax.shard_map(
        per_device,
        mesh=mesh,
        in_specs=placed,
        out_specs=(
            P("dp", "expert"),
            P("dp", "expert"),
            P("dp", None),
            P(("dp", "expert"), None, None),
            P(("dp", "expert"), None, None),
            P(("dp", "expert"), None, None),
        ),
        check_vma=False,
    )
```

```python
import jax
import jax.numpy as jnp
from jax import lax
from jax.sharding import PartitionSpec as P

SHARDS = 4


def silu_parts(preact):
    sigmoid_of = jax.nn.sigmoid(preact)
    activated = preact * sigmoid_of
    derivative = sigmoid_of * (1.0 + preact * (1.0 - sigmoid_of))
    return (activated, derivative)


def contract_last(first_op, second_op):
    return lax.dot_general(
        first_op, second_op, (((1,), (1,)), ((), ())), preferred_element_type=jnp.float32
    )


def contract_first(first_op, second_op):
    return lax.dot_general(
        first_op, second_op, (((0,), (0,)), ((), ())), preferred_element_type=jnp.float32
    )


def expert_rows(rows_x, rows_do, gate_w, up_w, down_w):
    pre_gate = contract_last(rows_x, gate_w)
    pre_up = contract_last(rows_x, up_w)
    activated, derivative = silu_parts(pre_gate)
    hidden = (activated * pre_up).astype(jnp.bfloat16)
    part_out = jnp.dot(hidden, down_w, preferred_element_type=jnp.float32).astype(jnp.bfloat16)
    d_hidden = contract_last(rows_do, down_w)
    d_pre_gate = (d_hidden * pre_up * derivative).astype(jnp.bfloat16)
    d_pre_up = (d_hidden * activated).astype(jnp.bfloat16)
    part_grad = (
        jnp.dot(d_pre_gate, gate_w, preferred_element_type=jnp.float32)
        + jnp.dot(d_pre_up, up_w, preferred_element_type=jnp.float32)
    ).astype(jnp.bfloat16)
    gradients = (
        contract_first(d_pre_gate, rows_x),
        contract_first(d_pre_up, rows_x),
        contract_first(hidden, rows_do),
    )
    return (part_out, part_grad, gradients)


def per_device(tokens, cotangent, expert_ids, gate_weights, w_gate, w_up, w_down):
    full_x = lax.all_gather(tokens, "expert", axis=1, tiled=True)
    full_dy = lax.all_gather(cotangent, "expert", axis=1, tiled=True)
    dp_count = lax.axis_size("dp")
    column_count = lax.axis_size("expert")
    column = lax.axis_index("expert")
    tok_count, chosen = expert_ids.shape
    features = full_x.shape[1]
    experts_all = dp_count * column_count // SHARDS
    capacity = min(tok_count, max(2, 2 * tok_count * chosen // experts_all))
    per_row = column_count // SHARDS
    assigned = tok_count * chosen
    flat_ids = expert_ids.reshape(-1)
    flat_gates = gate_weights.reshape(-1)
    slot_total = dp_count * capacity
    owned_here = flat_ids % per_row == column // SHARDS
    target_row = flat_ids // per_row
    onehot = (
        (target_row[:, None] == jnp.arange(dp_count, dtype=jnp.int32)[None, :])
        & owned_here[:, None]
    ).astype(jnp.bfloat16)
    order = jnp.arange(assigned, dtype=jnp.int32)
    earlier = (order[:, None] > order[None, :]).astype(jnp.bfloat16)
    counts = jnp.dot(earlier, onehot, preferred_element_type=jnp.float32)
    rank_of = jnp.sum(counts * onehot.astype(jnp.float32), axis=1).astype(jnp.int32)
    target = jnp.where(owned_here, target_row * capacity + rank_of, slot_total)
    picks = target[None, :] == jnp.arange(slot_total, dtype=jnp.int32)[:, None]
    slot_gate = jnp.sum(jnp.where(picks, flat_gates[None, :], 0.0), axis=1)
    token_of = jnp.any(picks.reshape(slot_total, tok_count, chosen), axis=2)
    token_pick = token_of.astype(jnp.bfloat16)
    send_x = jnp.dot(token_pick, full_x, preferred_element_type=jnp.bfloat16).reshape(
        dp_count, capacity, features
    )
    slot_dy = jnp.dot(token_pick, full_dy, preferred_element_type=jnp.float32)
    send_do = (
        (slot_gate[:, None] * slot_dy).astype(jnp.bfloat16).reshape(dp_count, capacity, features)
    )
    weights = (w_gate[0], w_up[0], w_down[0])
    recv_x = lax.all_to_all(send_x, "dp", split_axis=0, concat_axis=0, tiled=True)
    recv_do = lax.all_to_all(send_do, "dp", split_axis=0, concat_axis=0, tiled=True)
    rows_x = recv_x.reshape(slot_total, features)
    rows_do = recv_do.reshape(slot_total, features)
    part_out, part_grad, gradients = expert_rows(rows_x, rows_do, *weights)
    back = lax.all_to_all(
        jnp.concatenate(
            [
                part_out.reshape(dp_count, capacity, features),
                part_grad.reshape(dp_count, capacity, features),
            ],
            axis=1,
        ),
        "dp",
        split_axis=0,
        concat_axis=0,
        tiled=True,
    )
    back_out = back[:, :capacity].reshape(slot_total, features)
    back_grad = back[:, capacity:].reshape(slot_total, features)
    gated_pick = token_pick.astype(jnp.float32) * slot_gate[:, None]
    out_part = lax.dot_general(
        gated_pick,
        back_out.astype(jnp.float32),
        (((0,), (0,)), ((), ())),
        precision=lax.Precision.HIGHEST,
        preferred_element_type=jnp.float32,
    )
    grad_part = contract_first(token_pick, back_grad)
    dy_rows = jnp.dot(token_pick, full_dy, preferred_element_type=jnp.bfloat16)
    gate_terms = jnp.sum(dy_rows.astype(jnp.float32) * back_out.astype(jnp.float32), axis=1)
    gate_part = jnp.sum(jnp.where(picks, gate_terms[:, None], 0.0), axis=0).reshape(
        tok_count, chosen
    )
    summed = lax.psum_scatter(
        jnp.stack([out_part, grad_part]), "expert", scatter_dimension=2, tiled=True
    )
    gate_all = lax.all_gather(gate_part, "expert", axis=0, tiled=False)
    grad_gates = gate_all[0]
    for source in range(1, column_count):
        grad_gates = grad_gates + gate_all[source]
    return (
        summed[0].astype(jnp.bfloat16),
        summed[1].astype(jnp.bfloat16),
        grad_gates,
        gradients[0].astype(jnp.bfloat16)[None],
        gradients[1].astype(jnp.bfloat16)[None],
        gradients[2].astype(jnp.bfloat16)[None],
    )


def solution(mesh):
    placed = (
        P("dp", "expert"),
        P("dp", "expert"),
        P("dp", None),
        P("dp", None),
        P(("dp", "expert"), None, None),
        P(("dp", "expert"), None, None),
        P(("dp", "expert"), None, None),
    )
    return jax.shard_map(
        per_device,
        mesh=mesh,
        in_specs=placed,
        out_specs=(
            P("dp", "expert"),
            P("dp", "expert"),
            P("dp", None),
            P(("dp", "expert"), None, None),
            P(("dp", "expert"), None, None),
            P(("dp", "expert"), None, None),
        ),
        check_vma=False,
    )
```

```python
import jax
import jax.numpy as jnp
from jax import lax
from jax.sharding import PartitionSpec as P

SHARDS = 4


def silu_parts(preact):
    sigmoid_of = jax.nn.sigmoid(preact)
    activated = preact * sigmoid_of
    derivative = sigmoid_of * (1.0 + preact * (1.0 - sigmoid_of))
    return (activated, derivative)


def contract_last(first_op, second_op):
    return lax.dot_general(
        first_op, second_op, (((1,), (1,)), ((), ())), preferred_element_type=jnp.float32
    )


def contract_first(first_op, second_op):
    return lax.dot_general(
        first_op, second_op, (((0,), (0,)), ((), ())), preferred_element_type=jnp.float32
    )


def expert_rows(rows_x, rows_do, gate_w, up_w, down_w):
    pre_gate = contract_last(rows_x, gate_w)
    pre_up = contract_last(rows_x, up_w)
    activated, derivative = silu_parts(pre_gate)
    hidden = (activated * pre_up).astype(jnp.bfloat16)
    part_out = jnp.dot(hidden, down_w, preferred_element_type=jnp.float32).astype(jnp.bfloat16)
    d_hidden = contract_last(rows_do, down_w)
    d_pre_gate = (d_hidden * pre_up * derivative).astype(jnp.bfloat16)
    d_pre_up = (d_hidden * activated).astype(jnp.bfloat16)
    part_grad = (
        jnp.dot(d_pre_gate, gate_w, preferred_element_type=jnp.float32)
        + jnp.dot(d_pre_up, up_w, preferred_element_type=jnp.float32)
    ).astype(jnp.bfloat16)
    gradients = (
        contract_first(d_pre_gate, rows_x),
        contract_first(d_pre_up, rows_x),
        contract_first(hidden, rows_do),
    )
    return (part_out, part_grad, gradients)


def per_device(tokens, cotangent, expert_ids, gate_weights, w_gate, w_up, w_down):
    full_x = lax.all_gather(tokens, "expert", axis=1, tiled=True)
    full_dy = lax.all_gather(cotangent, "expert", axis=1, tiled=True)
    dp_count = lax.axis_size("dp")
    column_count = lax.axis_size("expert")
    column = lax.axis_index("expert")
    tok_count, chosen = expert_ids.shape
    features = full_x.shape[1]
    experts_all = dp_count * column_count // SHARDS
    capacity = min(tok_count, max(2, 2 * tok_count * chosen // experts_all))
    per_row = column_count // SHARDS
    assigned = tok_count * chosen
    flat_ids = expert_ids.reshape(-1)
    flat_gates = gate_weights.reshape(-1)
    slot_total = dp_count * capacity
    owned_here = flat_ids % per_row == column // SHARDS
    target_row = flat_ids // per_row
    onehot = (
        (target_row[:, None] == jnp.arange(dp_count, dtype=jnp.int32)[None, :])
        & owned_here[:, None]
    ).astype(jnp.bfloat16)
    order = jnp.arange(assigned, dtype=jnp.int32)
    earlier = (order[:, None] > order[None, :]).astype(jnp.bfloat16)
    counts = jnp.dot(earlier, onehot, preferred_element_type=jnp.float32)
    rank_of = jnp.sum(counts * onehot.astype(jnp.float32), axis=1).astype(jnp.int32)
    target = jnp.where(owned_here, target_row * capacity + rank_of, slot_total)
    picks = target[None, :] == jnp.arange(slot_total, dtype=jnp.int32)[:, None]
    slot_gate = jnp.sum(jnp.where(picks, flat_gates[None, :], 0.0), axis=1)
    token_of = jnp.any(picks.reshape(slot_total, tok_count, chosen), axis=2)
    token_pick = token_of.astype(jnp.bfloat16)
    send_x = jnp.dot(token_pick, full_x, preferred_element_type=jnp.bfloat16).reshape(
        dp_count, capacity, features
    )
    slot_dy = jnp.dot(token_pick, full_dy, preferred_element_type=jnp.float32)
    send_do = (
        (slot_gate[:, None] * slot_dy).astype(jnp.bfloat16).reshape(dp_count, capacity, features)
    )
    weights = (w_gate[0], w_up[0], w_down[0])
    recv_x = lax.all_to_all(send_x, "dp", split_axis=0, concat_axis=0, tiled=True)
    recv_do = lax.all_to_all(send_do, "dp", split_axis=0, concat_axis=0, tiled=True)
    rows_x = recv_x.reshape(slot_total, features)
    rows_do = recv_do.reshape(slot_total, features)
    part_out, part_grad, gradients = expert_rows(rows_x, rows_do, *weights)
    back = lax.all_to_all(
        jnp.concatenate(
            [
                part_out.reshape(dp_count, capacity, features),
                part_grad.reshape(dp_count, capacity, features),
            ],
            axis=1,
        ),
        "dp",
        split_axis=0,
        concat_axis=0,
        tiled=True,
    )
    back_out = back[:, :capacity].reshape(slot_total, features)
    back_grad = back[:, capacity:].reshape(slot_total, features)
    gate_hi = lax.reduce_precision(slot_gate, exponent_bits=8, mantissa_bits=7)
    gate_rest = slot_gate - gate_hi
    gate_mid = lax.reduce_precision(gate_rest, exponent_bits=8, mantissa_bits=7)
    gate_lo = gate_rest - gate_mid
    pick_float = token_pick.astype(jnp.float32)
    gate_cols = jnp.concatenate(
        [pick_float * gate_hi[:, None], pick_float * gate_mid[:, None], pick_float * gate_lo[:, None]],
        axis=1,
    ).astype(jnp.bfloat16)
    out_pieces = contract_first(gate_cols, back_out)
    out_part = (out_pieces[:tok_count] + out_pieces[tok_count : 2 * tok_count]) + out_pieces[
        2 * tok_count :
    ]
    grad_part = contract_first(token_pick, back_grad)
    dy_rows = jnp.dot(token_pick, full_dy, preferred_element_type=jnp.bfloat16)
    gate_terms = jnp.sum(dy_rows.astype(jnp.float32) * back_out.astype(jnp.float32), axis=1)
    gate_part = jnp.sum(jnp.where(picks, gate_terms[:, None], 0.0), axis=0).reshape(
        tok_count, chosen
    )
    summed = lax.psum_scatter(
        jnp.stack([out_part, grad_part]), "expert", scatter_dimension=2, tiled=True
    )
    gate_all = lax.all_gather(gate_part, "expert", axis=0, tiled=False)
    grad_gates = gate_all[0]
    for source in range(1, column_count):
        grad_gates = grad_gates + gate_all[source]
    return (
        summed[0].astype(jnp.bfloat16),
        summed[1].astype(jnp.bfloat16),
        grad_gates,
        gradients[0].astype(jnp.bfloat16)[None],
        gradients[1].astype(jnp.bfloat16)[None],
        gradients[2].astype(jnp.bfloat16)[None],
    )


def solution(mesh):
    placed = (
        P("dp", "expert"),
        P("dp", "expert"),
        P("dp", None),
        P("dp", None),
        P(("dp", "expert"), None, None),
        P(("dp", "expert"), None, None),
        P(("dp", "expert"), None, None),
    )
    return jax.shard_map(
        per_device,
        mesh=mesh,
        in_specs=placed,
        out_specs=(
            P("dp", "expert"),
            P("dp", "expert"),
            P("dp", None),
            P(("dp", "expert"), None, None),
            P(("dp", "expert"), None, None),
            P(("dp", "expert"), None, None),
        ),
        check_vma=False,
    )
```

```python
import jax
import jax.numpy as jnp
from jax import lax
from jax.sharding import PartitionSpec as P

SHARDS = 4


def silu_parts(preact):
    sigmoid_of = jax.nn.sigmoid(preact)
    activated = preact * sigmoid_of
    derivative = sigmoid_of * (1.0 + preact * (1.0 - sigmoid_of))
    return (activated, derivative)


def contract_last(first_op, second_op):
    return lax.dot_general(
        first_op, second_op, (((1,), (1,)), ((), ())), preferred_element_type=jnp.float32
    )


def contract_first(first_op, second_op):
    return lax.dot_general(
        first_op, second_op, (((0,), (0,)), ((), ())), preferred_element_type=jnp.float32
    )


def expert_rows(rows_x, rows_do, gate_w, up_w, down_w):
    pre_gate = contract_last(rows_x, gate_w)
    pre_up = contract_last(rows_x, up_w)
    activated, derivative = silu_parts(pre_gate)
    hidden = (activated * pre_up).astype(jnp.bfloat16)
    part_out = jnp.dot(hidden, down_w, preferred_element_type=jnp.float32).astype(jnp.bfloat16)
    d_hidden = contract_last(rows_do, down_w)
    d_pre_gate = (d_hidden * pre_up * derivative).astype(jnp.bfloat16)
    d_pre_up = (d_hidden * activated).astype(jnp.bfloat16)
    part_grad = (
        jnp.dot(d_pre_gate, gate_w, preferred_element_type=jnp.float32)
        + jnp.dot(d_pre_up, up_w, preferred_element_type=jnp.float32)
    ).astype(jnp.bfloat16)
    gradients = (
        contract_first(d_pre_gate, rows_x),
        contract_first(d_pre_up, rows_x),
        contract_first(hidden, rows_do),
    )
    return (part_out, part_grad, gradients)


def forward_part(rows_x, gate_w, up_w, down_w):
    pre_gate = contract_last(rows_x, gate_w)
    pre_up = contract_last(rows_x, up_w)
    activated, derivative = silu_parts(pre_gate)
    hidden = (activated * pre_up).astype(jnp.bfloat16)
    part_out = jnp.dot(hidden, down_w, preferred_element_type=jnp.float32).astype(jnp.bfloat16)
    return (pre_up, activated, derivative, hidden, part_out)


def backward_part(rows_x, rows_do, gate_w, up_w, down_w, pre_up, activated, derivative, hidden):
    d_hidden = contract_last(rows_do, down_w)
    d_pre_gate = (d_hidden * pre_up * derivative).astype(jnp.bfloat16)
    d_pre_up = (d_hidden * activated).astype(jnp.bfloat16)
    part_grad = (
        jnp.dot(d_pre_gate, gate_w, preferred_element_type=jnp.float32)
        + jnp.dot(d_pre_up, up_w, preferred_element_type=jnp.float32)
    ).astype(jnp.bfloat16)
    gradients = (
        contract_first(d_pre_gate, rows_x),
        contract_first(d_pre_up, rows_x),
        contract_first(hidden, rows_do),
    )
    return (part_grad, gradients)


def per_device(tokens, cotangent, expert_ids, gate_weights, w_gate, w_up, w_down):
    full_x = lax.all_gather(tokens, "expert", axis=1, tiled=True)
    full_dy = lax.all_gather(cotangent, "expert", axis=1, tiled=True)
    dp_count = lax.axis_size("dp")
    column_count = lax.axis_size("expert")
    column = lax.axis_index("expert")
    tok_count, chosen = expert_ids.shape
    features = full_x.shape[1]
    experts_all = dp_count * column_count // SHARDS
    capacity = min(tok_count, max(2, 2 * tok_count * chosen // experts_all))
    per_row = column_count // SHARDS
    assigned = tok_count * chosen
    flat_ids = expert_ids.reshape(-1)
    flat_gates = gate_weights.reshape(-1)
    slot_total = dp_count * capacity
    owned_here = flat_ids % per_row == column // SHARDS
    target_row = flat_ids // per_row
    onehot = (
        (target_row[:, None] == jnp.arange(dp_count, dtype=jnp.int32)[None, :])
        & owned_here[:, None]
    ).astype(jnp.bfloat16)
    order = jnp.arange(assigned, dtype=jnp.int32)
    earlier = (order[:, None] > order[None, :]).astype(jnp.bfloat16)
    counts = jnp.dot(earlier, onehot, preferred_element_type=jnp.float32)
    rank_of = jnp.sum(counts * onehot.astype(jnp.float32), axis=1).astype(jnp.int32)
    target = jnp.where(owned_here, target_row * capacity + rank_of, slot_total)
    picks = target[None, :] == jnp.arange(slot_total, dtype=jnp.int32)[:, None]
    slot_gate = jnp.sum(jnp.where(picks, flat_gates[None, :], 0.0), axis=1)
    token_of = jnp.any(picks.reshape(slot_total, tok_count, chosen), axis=2)
    token_pick = token_of.astype(jnp.bfloat16)
    send_x = jnp.dot(token_pick, full_x, preferred_element_type=jnp.bfloat16).reshape(
        dp_count, capacity, features
    )
    slot_dy = jnp.dot(token_pick, full_dy, preferred_element_type=jnp.float32)
    send_do = (
        (slot_gate[:, None] * slot_dy).astype(jnp.bfloat16).reshape(dp_count, capacity, features)
    )
    weights = (w_gate[0], w_up[0], w_down[0])
    recv_x = lax.all_to_all(send_x, "dp", split_axis=0, concat_axis=0, tiled=True)
    recv_do = lax.all_to_all(send_do, "dp", split_axis=0, concat_axis=0, tiled=True)
    rows_x = recv_x.reshape(slot_total, features)
    rows_do = recv_do.reshape(slot_total, features)
    pre_up, activated, derivative, hidden, part_out = forward_part(rows_x, *weights)
    part_out, hidden, rows_do = lax.optimization_barrier((part_out, hidden, rows_do))
    part_grad, gradients = backward_part(
        rows_x, rows_do, *weights, pre_up, activated, derivative, hidden
    )
    back = lax.all_to_all(
        jnp.concatenate(
            [
                part_out.reshape(dp_count, capacity, features),
                part_grad.reshape(dp_count, capacity, features),
            ],
            axis=1,
        ),
        "dp",
        split_axis=0,
        concat_axis=0,
        tiled=True,
    )
    back_out = back[:, :capacity].reshape(slot_total, features)
    back_grad = back[:, capacity:].reshape(slot_total, features)
    gated_pick = token_pick.astype(jnp.float32) * slot_gate[:, None]
    out_part = lax.dot_general(
        gated_pick,
        back_out.astype(jnp.float32),
        (((0,), (0,)), ((), ())),
        precision=lax.Precision.HIGHEST,
        preferred_element_type=jnp.float32,
    )
    grad_part = contract_first(token_pick, back_grad)
    dy_rows = jnp.dot(token_pick, full_dy, preferred_element_type=jnp.bfloat16)
    gate_terms = jnp.sum(dy_rows.astype(jnp.float32) * back_out.astype(jnp.float32), axis=1)
    gate_part = jnp.sum(jnp.where(picks, gate_terms[:, None], 0.0), axis=0).reshape(
        tok_count, chosen
    )
    summed = lax.psum_scatter(
        jnp.stack([out_part, grad_part]), "expert", scatter_dimension=2, tiled=True
    )
    gate_all = lax.all_gather(gate_part, "expert", axis=0, tiled=False)
    grad_gates = gate_all[0]
    for source in range(1, column_count):
        grad_gates = grad_gates + gate_all[source]
    return (
        summed[0].astype(jnp.bfloat16),
        summed[1].astype(jnp.bfloat16),
        grad_gates,
        gradients[0].astype(jnp.bfloat16)[None],
        gradients[1].astype(jnp.bfloat16)[None],
        gradients[2].astype(jnp.bfloat16)[None],
    )


def solution(mesh):
    placed = (
        P("dp", "expert"),
        P("dp", "expert"),
        P("dp", None),
        P("dp", None),
        P(("dp", "expert"), None, None),
        P(("dp", "expert"), None, None),
        P(("dp", "expert"), None, None),
    )
    return jax.shard_map(
        per_device,
        mesh=mesh,
        in_specs=placed,
        out_specs=(
            P("dp", "expert"),
            P("dp", "expert"),
            P("dp", None),
            P(("dp", "expert"), None, None),
            P(("dp", "expert"), None, None),
            P(("dp", "expert"), None, None),
        ),
        check_vma=False,
    )
```
